512 devices in a mesh: row: 32 (over x_lo, z), col: 8 (over y, core), rep: 2 (over x_hi).
Axes of the slice: x: 4 (x_hi: 2, x_lo: 2; x = x_hi * 2 + x_lo), y: 4, z: 16, core: 2. Of those that a mesh axis runs over, the one named last changes fastest.
Arguments:
- adj_tiles: float32 [32, 8, 4, 512, 512], P('row', 'col'), may hold values from -0.25 to 0.25
- tile_rows: int32 [32, 8, 4], P('row', 'col'), may hold values from 0 to 7
- tile_cols: int32 [32, 8, 4], P('row', 'col'), may hold values from 0 to 31
- tile_counts: int32 [32, 8], P('row', 'col'), may hold values from 1 to 4, as said below
- features_t: float32 [128, 131072], P('rep', ('row', 'col')), may hold values from -6 to 6
- weight: float32 [128, 128], P('rep'), may hold values from -0.5 to 0.5
- bias_vec: float32 [128], replicated, may hold values from -3 to 3
- cotangent: float32 [131072, 128], P(('row', 'col', 'rep')), may hold values from -0.02 to 0.02
Outputs:
- output: float32 [131072, 128], P(('row', 'col', 'rep'))
- grad_weight: float32 [128, 128], P('rep')
- grad_bias: float32 [128], replicated
The draws below stay inside these ranges and needn't reach their ends.
Inputs may be any that keep to these rules, and one draw needn't show every extreme that they name: `tile_counts`: the number of live slots of each cell; some cell has all 4 slots live. `tile_rows`: block row of a slot inside its row group; dead slots hold arbitrary values. `tile_cols`: block column of a slot inside its column group; dead slots hold arbitrary values.
All inputs are finite; a program needn't handle non-finite values.
Results may differ from the reference program's by a relative error of at most 0.0001.
Values sent between devices are 32-bit elements; how exact they have to be, the bound alone decides.
A program may use at most 64 MiB of HBM per device.

```python
import jax
import jax.numpy as jnp
from jax import lax

F = 128
BLOCK = 512
TILES_DEV = 4
NODES = 131072
N_ROW = 32
N_COL = 8


def draw_tile_counts(key, part):
    first_key = jax.random.fold_in(key, 11)
    second_key = jax.random.fold_in(key, 23)
    counts_flat = jax.random.randint(first_key, (N_ROW * N_COL,), 1, TILES_DEV + 1)
    chosen = jax.random.randint(second_key, (), 0, N_ROW * N_COL)
    counts_flat = counts_flat.at[chosen].set(TILES_DEV)
    return counts_flat.reshape(N_ROW, N_COL).astype(jnp.int32)


def place_ends(array, key, smallest, top_value):
    longest = array.shape.index(max(array.shape))
    spots = []
    for shift in (0, 1):
        where = [jax.random.randint(jax.random.fold_in(key, axis), (), 0, length) for axis, length in enumerate(array.shape)]
        where[longest] = (where[longest] + shift) % array.shape[longest]
        spots.append(tuple(where))
    return array.at[spots[0]].set(smallest).at[spots[1]].set(top_value)


def block_scale(own_key, dims, shards, low, high):
    def one(dim, blocks):
        heights = jax.random.uniform(jax.random.fold_in(jax.random.fold_in(own_key, 6), dim), (blocks,), jnp.float32, low / len(shards), high / len(shards))
        return jnp.repeat(jnp.exp(heights), dims[dim] // blocks).reshape((-1,) + (1,) * (len(dims) - dim - 1))

    gain = one(*shards[0])
    for cut in shards[1:]:
        gain = gain * one(*cut)
    return gain


def noise(key, dims, deviation, reach, cuts=(), held_as=jnp.bfloat16):
    array = deviation * jax.random.normal(key, dims, jnp.float32)
    if cuts:
        array = array * block_scale(key, dims, cuts, -0.22, 0.18)
    return jnp.clip(array, -reach, reach).astype(held_as)


def setup_inputs(seed: int = 0) -> dict:
    arg_keys = jax.random.split(jax.random.key(seed), 9)
    return {
        "adj_tiles": noise(arg_keys[0], (N_ROW, N_COL, TILES_DEV, BLOCK, BLOCK), BLOCK ** -0.5, 0.25, ((0, 32), (1, 8)), jnp.float32),
        "tile_rows": place_ends(jax.random.randint(arg_keys[1], (N_ROW, N_COL, TILES_DEV), 0, N_COL), jax.random.fold_in(arg_keys[1], 1), 0, N_COL - 1).astype(jnp.int32),
        "tile_cols": place_ends(jax.random.randint(arg_keys[2], (N_ROW, N_COL, TILES_DEV), 0, N_ROW), jax.random.fold_in(arg_keys[2], 1), 0, N_ROW - 1).astype(jnp.int32),
        "tile_counts": draw_tile_counts(jax.random.fold_in(arg_keys[8], 71), 0),
        "features_t": noise(arg_keys[4], (F, NODES), 1.0, 6.0, ((0, 2), (1, 256)), jnp.float32),
        "weight": noise(arg_keys[5], (F, F), F ** -0.5, 0.5, ((0, 2),), jnp.float32),
        "bias_vec": noise(arg_keys[6], (F,), 0.5, 3.0, (), jnp.float32),
        "cotangent": noise(arg_keys[7], (NODES, F), 0.003, 0.02, ((0, 512),), jnp.float32),
    }


def reference(adj_tiles, tile_rows, tile_cols, tile_counts, features_t, weight, bias_vec, cotangent):
    row_groups, col_groups, slot_count = tile_rows.shape
    block_len = adj_tiles.shape[-1]
    width = features_t.shape[0]
    node_feats = features_t.T.reshape(-1, block_len, width)
    row_global = (jnp.arange(row_groups, dtype=jnp.int32)[:, None, None] * col_groups + tile_rows).reshape(-1).astype(jnp.int32)
    col_global = (tile_cols * col_groups + jnp.arange(col_groups, dtype=jnp.int32)[None, :, None]).reshape(-1).astype(jnp.int32)
    is_live = (jnp.arange(slot_count, dtype=jnp.int32)[None, None, :] < tile_counts[:, :, None]).reshape(-1)
    flat_tiles = adj_tiles.reshape(-1, block_len, block_len)

    def add_tile(running, item):
        slab_one, row_block, col_block, usable = item
        contrib = jnp.dot(slab_one, node_feats[col_block], precision=lax.Precision.HIGHEST, preferred_element_type=jnp.float32)
        contrib = jnp.where(usable, contrib, jnp.zeros_like(contrib))
        return running.at[row_block].add(contrib), None

    start_sum = jnp.zeros(node_feats.shape, jnp.float32)
    summed, _ = lax.scan(add_tile, start_sum, (flat_tiles, row_global, col_global, is_live))
    mixed = summed.reshape(-1, width)
    preact = jnp.dot(mixed, weight, precision=lax.Precision.HIGHEST, preferred_element_type=jnp.float32) + bias_vec
    squash = jax.nn.sigmoid(preact)
    output = preact * squash
    slope = cotangent * squash * (1.0 + preact * (1.0 - squash))
    grad_weight = jnp.dot(mixed.T, slope, precision=lax.Precision.HIGHEST, preferred_element_type=jnp.float32)
    grad_bias = jnp.sum(slope, axis=0)
    return output, grad_weight, grad_bias
```

```python
import functools

import jax
import jax.numpy as jnp
from jax import lax
from jax.experimental import pallas as pl
from jax.experimental.pallas import tpu as pltpu
from jax.sharding import PartitionSpec as P

MESH = pl.DeviceIdType.MESH
F32 = jnp.float32
BF16 = jnp.bfloat16
HIGHEST = lax.Precision.HIGHEST

NY = 4
CHIPS = 16
OVER_X = 40
OFFSETS = (2, 1, 3, 0)


def remote(src, dst, send_sem, recv_sem, device):
    return pltpu.make_async_remote_copy(
        src_ref=src, dst_ref=dst, send_sem=send_sem, recv_sem=recv_sem, device_id=device, device_id_type=MESH
    )


def kernel(
    nz,
    rows_ref, cols_ref, counts_ref, adj_ref, feat_ref, weight_ref, bias_ref, cot_ref,
    out_ref, gw_ref, gb_ref,
    gath, adj_in, adj_hi, adj_lo, prod, m_out, c1_in, s_buf,
    relay, direct, mid, final, away, mt, w_full, cot, out_v,
    g_buf, f1_in, f2_in, f3_in, p2, p3, b_one, b_two, b1_in, b2_in, b3_in,
    zr, xr, xo, zs, xs, lsem, asem, wsem, csem, ysem, ysend, dsem, fsem,
):
    row, col, rep = lax.axis_index("row"), lax.axis_index("col"), lax.axis_index("rep")
    x_lo, z = row // nz, row % nz
    y, core = col // 2, col % 2
    far = nz // 2
    width, block = feat_ref.shape
    half_w, half_b = width // 2, block // 2
    keep = width - OVER_X

    z_dev = ({"row": x_lo * nz + (z + 1) % nz}, {"row": x_lo * nz + (z + nz - 1) % nz})
    x_dev = {"row": (1 - x_lo) * nz + z}
    core_dev = {"col": y * 2 + 1 - core}
    y_dev = ({"col": ((y + 1) % NY) * 2 + core}, {"col": ((y + NY - 1) % NY) * 2 + core})
    rep_dev = {"rep": 1 - rep}

    barrier = pltpu.get_barrier_semaphore()
    for device in (*z_dev, x_dev, core_dev, *y_dev, rep_dev):
        pl.semaphore_signal(barrier, inc=1, device_id=device, device_id_type=MESH)

    adj_copies = [pltpu.make_async_copy(adj_ref.at[0, 0, t], adj_in.at[t], asem.at[t]) for t in range(4)]
    own_copy = pltpu.make_async_copy(feat_ref, gath.at[row], lsem.at[0])
    cot_copy = pltpu.make_async_copy(cot_ref, cot, lsem.at[1])
    w_copy = pltpu.make_async_copy(weight_ref, w_full.at[pl.ds(rep * width, width)], lsem.at[2])

    pl.semaphore_wait(barrier, 7)

    def slot(plane, hops, way):
        return plane * nz + (z + nz - hops if way == 0 else z + hops) % nz

    def over_z(plane, hops, way, low, count, part, first=False):
        place = slot(plane, hops - 1, way)
        source = feat_ref if first else gath.at[place]
        return remote(
            source.at[pl.ds(low, count)],
            gath.at[place, pl.ds(low, count)],
            zs.at[0 if part < 2 else (1 if hops < far else 2)],
            zr.at[way, hops - 1, part],
            z_dev[way],
        )

    def landed_z(plane, hops, way, low, count, part):
        place = gath.at[slot(plane, hops, way), pl.ds(low, count)]
        remote(place, place, zs.at[0], zr.at[way, hops - 1, part], z_dev[way]).wait_recv()

    def over_x(hops, way):
        piece = gath.at[slot(x_lo, hops, way), pl.ds(0, OVER_X)]
        return remote(piece, piece, xs.at[1], xr.at[way, hops - 1], x_dev)

    def landed_x(hops, way):
        piece = gath.at[slot(1 - x_lo, hops, way), pl.ds(0, OVER_X)]
        remote(piece, piece, xs.at[1], xr.at[way, hops - 1], x_dev).wait_recv()

    def own_over_x(low, count, which, place):
        return remote(
            feat_ref.at[pl.ds(low, count)], gath.at[place, pl.ds(low, count)], xs.at[0], xo.at[which], x_dev
        )

    own_over_x(OVER_X, keep, 1, row).start()
    for way in (0, 1):
        over_z(x_lo, 1, way, 0, OVER_X, 0, True).start()
    for way in (0, 1):
        over_z(x_lo, 1, way, OVER_X, keep, 1, True).start()
    own_over_x(0, OVER_X, 0, row).start()
    for copy in (own_copy, *adj_copies, cot_copy, w_copy):
        copy.start()
    w_send = remote(weight_ref, w_full.at[pl.ds(rep * width, width)], wsem.at[0], wsem.at[1], rep_dev)
    w_send.start()

    chunk = 32
    chunks = block // chunk * 4

    def split(first, count):
        def one(i, carry):
            t, low = i // (block // chunk), pl.multiple_of((i % (block // chunk)) * chunk, chunk)
            value = adj_in[t, pl.ds(low, chunk), :]
            high = value.astype(BF16)
            adj_hi[t, pl.ds(low, chunk), :] = high
            adj_lo[t, pl.ds(low, chunk), :] = (value - high.astype(F32)).astype(BF16)
            return carry

        lax.fori_loop(first, first + count, one, 0)

    partner = (1 - x_lo) * nz + z
    own_over_x(OVER_X, keep, 1, partner).wait_recv()
    for way in (0, 1):
        over_z(1 - x_lo, 1, way, OVER_X, keep, 2).start()
    done = 0
    for hops in range(1, far):
        last = hops == far - 1
        for way in (0, 1):
            landed_z(x_lo, hops, way, 0, OVER_X, 0)
            if not last:
                over_z(x_lo, hops + 1, way, 0, OVER_X, 0).start()
            over_x(hops, way).start()
            if last and way == 0:
                over_z(x_lo, far, 0, 0, half_w, 0).start()
        for way in (0, 1):
            landed_z(x_lo, hops, way, OVER_X, keep, 1)
            if not last:
                over_z(x_lo, hops + 1, way, OVER_X, keep, 1).start()
            elif way == 1:
                over_z(x_lo, far, 1, half_w, half_w, 0).start()
        for way in (0, 1):
            landed_z(1 - x_lo, hops, way, OVER_X, keep, 2)
            if not last:
                over_z(1 - x_lo, hops + 1, way, OVER_X, keep, 2).start()
        if last:
            for way in (0, 1):
                landed_x(hops, way)
                over_z(1 - x_lo, far, way, way * half_w, half_w, 2).start()
        if hops == 1:
            for copy in adj_copies:
                copy.wait()
        upto = chunks * hops // (far - 1)
        split(done, upto - done)
        done = upto
    own_over_x(0, OVER_X, 0, partner).wait_recv()
    for hops in range(1, far - 1):
        for way in (0, 1):
            landed_x(hops, way)
    for copy in (own_copy, cot_copy, w_copy):
        copy.wait()
    for way in (0, 1):
        landed_z(x_lo, far, way, way * half_w, half_w, 0)
        landed_z(1 - x_lo, far, way, way * half_w, half_w, 2)

    count = counts_ref[0, 0]
    for t in range(4):
        value = gath[jnp.clip(cols_ref[0, 0, t], 0, 2 * nz - 1)]
        high = value.astype(BF16)
        low = (value - high.astype(F32)).astype(BF16)
        dims = (((1,), (1,)), ((), ()))
        both = lax.dot_general(jnp.concatenate([high, low], axis=0), adj_hi[t], dims, preferred_element_type=F32)
        rest = lax.dot_general(high, adj_lo[t], dims, preferred_element_type=F32)
        prod[t] = both[:width] + both[width:] + rest

    def placed(group):
        total = None
        for t in range(4):
            scale = jnp.where((t < count) & (rows_ref[0, 0, t] == group), F32(1.0), F32(0.0))
            term = prod[t] * scale
            total = term if total is None else total + term
        return total

    core_copies = []
    for k, offset in enumerate(OFFSETS):
        total = placed(((y + offset) % NY) * 2 + 1 - core)
        for h in (0, 1):
            m_out[k, h] = total[:, h * half_b : (h + 1) * half_b]
        copy = remote(m_out.at[k], c1_in.at[k], csem.at[0, k], csem.at[1, k], core_dev)
        copy.start()
        core_copies.append(copy)
    order = ((0, 1 - rep), (1, rep))
    up, down = pl.ds(0, half_w), pl.ds(half_w, half_w)
    y_copies = {}

    def over_y(src, dst, name, n, way):
        index = ("relay0", "relay1", "direct0", "direct1", "final0", "final1").index(name) * 2 + n
        copy = remote(src, dst, ysend.at[index], ysem.at[index], y_dev[way])
        copy.start()
        y_copies[name, n] = copy

    for k, offset in enumerate(OFFSETS):
        total = placed(((y + offset) % NY) * 2 + core)
        core_copies[k].wait_recv()
        for h in (0, 1):
            s_buf[k, h] = total[:, h * half_b : (h + 1) * half_b] + c1_in[k, h]
        for n, h in order:
            if offset == 2:
                over_y(s_buf.at[k, h, up], relay.at[0, n], "relay0", n, 0)
                over_y(s_buf.at[k, h, down], relay.at[1, n], "relay1", n, 1)
            elif offset == 1:
                over_y(s_buf.at[k, h, down], direct.at[1, n], "direct1", n, 0)
            elif offset == 3:
                over_y(s_buf.at[k, h, up], direct.at[0, n], "direct0", n, 1)
    for n, h in order:
        y_copies["relay0", n].wait_recv()
        mid[0, n] = relay[0, n] + s_buf[1, h, up]
        over_y(mid.at[0, n], final.at[0, n], "final0", n, 0)
        y_copies["relay1", n].wait_recv()
        mid[1, n] = relay[1, n] + s_buf[2, h, down]
        over_y(mid.at[1, n], final.at[1, n], "final1", n, 1)
    away_copy = remote(away, mt.at[pl.ds(rep * width, width)], dsem.at[0], dsem.at[1], rep_dev)
    for n, h in order:
        for part in (0, 1):
            y_copies["direct%d" % part, n].wait_recv()
            y_copies["final%d" % part, n].wait_recv()
            rows = pl.ds(part * half_w, half_w)
            total = s_buf[3, h, rows] + final[part, n] + direct[part, n]
            if n == 0:
                away[rows] = total
            else:
                mt[pl.ds(pl.multiple_of(rep * width + part * half_w, half_w), half_w), :] = total
        if n == 0:
            away_copy.start()
    w_send.wait_recv()
    away_copy.wait_recv()

    preact = jnp.dot(mt[...].T, w_full[...], precision=HIGHEST, preferred_element_type=F32) + bias_ref[...]
    squash = 1.0 / (1.0 + jnp.exp(-preact))
    out_v[...] = preact * squash
    out_copy = pltpu.make_async_copy(out_v, out_ref, lsem.at[3])
    out_copy.start()
    slope = cot[...] * squash * (1.0 + preact * (1.0 - squash))
    grad = jnp.dot(mt[...], slope, precision=HIGHEST, preferred_element_type=F32)
    g_buf[...] = grad.reshape(CHIPS, 8, 128)
    b_one[...] = jnp.sum(slope, axis=0, keepdims=True)

    me = rep * 8 + x_lo * 4 + y
    f1 = []
    for j in range(1, CHIPS):
        peer = (me + j) % CHIPS
        device = {"row": ((peer // 4) % 2) * nz + z, "col": (peer % 4) * 2 + core, "rep": peer // 8}
        f1.append(remote(g_buf.at[peer], f1_in.at[j - 1], fsem.at[0], fsem.at[1], device))
        f1.append(remote(b_one, b1_in.at[j - 1], fsem.at[2], fsem.at[3], device))
    for copy in f1:
        copy.start()
    remote(f1_in, f1_in, fsem.at[0], fsem.at[1], rep_dev).wait_recv()
    remote(b1_in, b1_in, fsem.at[2], fsem.at[3], rep_dev).wait_recv()
    mine = jnp.sum(f1_in[...], axis=0) + g_buf[me]
    bias_sum = jnp.sum(b1_in[...], axis=0) + b_one[...]
    p2[...] = mine
    f2_in[z] = mine
    b_two[...] = bias_sum
    b2_in[z] = bias_sum
    for k in sorted(range(1, nz), key=lambda j: -min(j, nz - j)):
        device = {"row": x_lo * nz + (z + k) % nz}
        remote(p2, f2_in.at[z], fsem.at[4], fsem.at[5], device).start()
        remote(b_two, b2_in.at[z], fsem.at[6], fsem.at[7], device).start()
    others = pl.ds(0, nz - 1)
    remote(f2_in.at[others], f2_in.at[others], fsem.at[4], fsem.at[5], rep_dev).wait()
    remote(b2_in.at[others], b2_in.at[others], fsem.at[6], fsem.at[7], rep_dev).wait()
    mine = jnp.sum(f2_in[...], axis=0)
    bias_sum = jnp.sum(b2_in[...], axis=0)
    p3[...] = mine
    place = x_lo * 4 + y
    f3_in[core, place] = mine
    b_two[...] = bias_sum
    b3_in[core] = bias_sum
    here = core * 8 + place
    for j in range(1, 16):
        peer = (here + j) % 16
        device = {"row": ((peer // 4) % 2) * nz + z, "col": (peer % 4) * 2 + peer // 8}
        remote(p3, f3_in.at[core, place], fsem.at[8], fsem.at[9], device).start()
    b3 = remote(b_two, b3_in.at[core], fsem.at[10], fsem.at[11], core_dev)
    b3.start()
    remote(f1_in, f1_in, fsem.at[8], fsem.at[9], rep_dev).wait()
    b3.wait()
    gw_ref[...] = (f3_in[0] + f3_in[1]).reshape(width, 128)
    gb_ref[...] = b3_in[0] + b3_in[1]

    out_copy.wait()
    remote(gath.at[pl.ds(0, nz - 1)], gath.at[pl.ds(0, nz - 1)], zs.at[0], zr.at[0, 0, 0], rep_dev).wait_send()
    part = gath.at[pl.ds(0, nz - 2), pl.ds(0, keep)]
    remote(part, part, zs.at[1], zr.at[0, 0, 0], rep_dev).wait_send()
    remote(gath.at[0], gath.at[0], zs.at[2], zr.at[0, 0, 0], rep_dev).wait_send()
    remote(gath.at[0], gath.at[0], xs.at[0], xr.at[0, 0], rep_dev).wait_send()
    part = gath.at[pl.ds(0, nz - 2), pl.ds(0, OVER_X)]
    remote(part, part, xs.at[1], xr.at[0, 0], rep_dev).wait_send()
    w_send.wait_send()
    away_copy.wait_send()
    for copy in (*core_copies, *y_copies.values()):
        copy.wait_send()
    remote(f1_in, f1_in, fsem.at[0], fsem.at[1], rep_dev).wait_send()
    remote(b1_in, b1_in, fsem.at[2], fsem.at[3], rep_dev).wait_send()


def solution(mesh):
    nz = mesh.shape["row"] // 2

    def local(adj_tiles, tile_rows, tile_cols, tile_counts, features_t, weight, bias_vec, cotangent):
        width, block = features_t.shape
        half_w, half_b = width // 2, block // 2
        out_w = weight.shape[1]
        nodes = cotangent.shape[0]
        smem = pl.BlockSpec(memory_space=pltpu.SMEM)
        vmem = pl.BlockSpec(memory_space=pltpu.VMEM)
        hbm = pl.BlockSpec(memory_space=pl.ANY)
        dma = pltpu.SemaphoreType.DMA
        output, grad_weight, grad_bias = pl.pallas_call(
            functools.partial(kernel, nz),
            out_shape=(
                jax.ShapeDtypeStruct((nodes, out_w), F32),
                jax.ShapeDtypeStruct((width, out_w), F32),
                jax.ShapeDtypeStruct((1, out_w), F32),
            ),
            in_specs=[smem, smem, smem, hbm, hbm, hbm, vmem, hbm],
            out_specs=(hbm, vmem, vmem),
            scratch_shapes=[
                pltpu.VMEM((2 * nz, width, block), F32),
                pltpu.VMEM((4, block, block), F32),
                pltpu.VMEM((4, block, block), BF16),
                pltpu.VMEM((4, block, block), BF16),
                pltpu.VMEM((4, width, block), F32),
                pltpu.VMEM((4, 2, width, half_b), F32),
                pltpu.VMEM((4, 2, width, half_b), F32),
                pltpu.VMEM((4, 2, width, half_b), F32),
                pltpu.VMEM((2, 2, half_w, half_b), F32),
                pltpu.VMEM((2, 2, half_w, half_b), F32),
                pltpu.VMEM((2, 2, half_w, half_b), F32),
                pltpu.VMEM((2, 2, half_w, half_b), F32),
                pltpu.VMEM((width, half_b), F32),
                pltpu.VMEM((2 * width, half_b), F32),
                pltpu.VMEM((2 * width, out_w), F32),
                pltpu.VMEM((nodes, out_w), F32),
                pltpu.VMEM((nodes, out_w), F32),
                pltpu.VMEM((CHIPS, 8, out_w), F32),
                pltpu.VMEM((CHIPS - 1, 8, out_w), F32),
                pltpu.VMEM((nz, 8, out_w), F32),
                pltpu.VMEM((2, 8, 8, out_w), F32),
                pltpu.VMEM((8, out_w), F32),
                pltpu.VMEM((8, out_w), F32),
                pltpu.VMEM((1, out_w), F32),
                pltpu.VMEM((1, out_w), F32),
                pltpu.VMEM((CHIPS - 1, 1, out_w), F32),
                pltpu.VMEM((nz, 1, out_w), F32),
                pltpu.VMEM((2, 1, out_w), F32),
                dma((2, nz // 2, 3)),
                dma((2, nz // 2)),
                dma((2,)),
                dma((3,)),
                dma((2,)),
                dma((4,)),
                dma((4,)),
                dma((2,)),
                dma((2, 4)),
                dma((12,)),
                dma((12,)),
                dma((2,)),
                dma((12,)),
            ],
            compiler_params=pltpu.CompilerParams(
                collective_id=0, has_side_effects=True, vmem_limit_bytes=48 * 1024 * 1024
            ),
        )(tile_rows, tile_cols, tile_counts, adj_tiles, features_t, weight, bias_vec.reshape(1, out_w), cotangent)
        return output, grad_weight, grad_bias.reshape(out_w)

    return jax.shard_map(
        local,
        mesh=mesh,
        in_specs=(
            P("row", "col", None, None, None),
            P("row", "col", None),
            P("row", "col", None),
            P("row", "col"),
            P("rep", ("row", "col")),
            P("rep", None),
            P(),
            P(("row", "col", "rep"), None),
        ),
        out_specs=(P(("row", "col", "rep"), None), P("rep", None), P()),
        check_vma=False,
    )
```

```python
import functools

import jax
import jax.numpy as jnp
from jax import lax
from jax.experimental import pallas as pl
from jax.experimental.pallas import tpu as pltpu
from jax.sharding import PartitionSpec as P

MESH = pl.DeviceIdType.MESH
F32 = jnp.float32
BF16 = jnp.bfloat16
HIGHEST = lax.Precision.HIGHEST

NY = 4
PIECES = 32
CHUNK = 16
OWN_ORDER = (2, 0, 1, 3)
OFFSETS = (2, 1, 3, 0)


def remote(src, dst, send_sem, recv_sem, device):
    return pltpu.make_async_remote_copy(
        src_ref=src, dst_ref=dst, send_sem=send_sem, recv_sem=recv_sem, device_id=device, device_id_type=MESH
    )


def kernel(
    nz,
    rows_ref, cols_ref, counts_ref, adj_ref, feat_ref, weight_ref, bias_ref, cot_ref,
    out_ref, gw_ref, gb_ref,
    rows_at, cols, counts, bias, gath, adj_in, adj_hi, adj_lo, prod, m_out, c1_in, s_buf,
    relay, direct, mid, final, away, mt, w_full, cot, out_v,
    g_buf, f1_in, f2_in, f3_in, p2, p3, b_one, b_two, b1_in, b2_in,
    zr, xr, xo, zs, xs, lsem, asem, wsem, csem, ysem, ysend, dsem, fsem,
):
    row, col, rep = lax.axis_index("row"), lax.axis_index("col"), lax.axis_index("rep")
    x_lo, z = row // nz, row % nz
    y, core = col // 2, col % 2
    far = nz // 2
    width, block = feat_ref.shape
    half_w, half_b = width // 2, block // 2

    z_dev = ({"row": x_lo * nz + (z + 1) % nz}, {"row": x_lo * nz + (z + nz - 1) % nz})
    x_dev = {"row": (1 - x_lo) * nz + z}
    core_dev = {"col": y * 2 + 1 - core}
    y_dev = ({"col": ((y + 1) % NY) * 2 + core}, {"col": ((y + NY - 1) % NY) * 2 + core})
    rep_dev = {"rep": 1 - rep}

    barrier = pltpu.get_barrier_semaphore()
    for device in (*z_dev, x_dev, core_dev, *y_dev, rep_dev):
        pl.semaphore_signal(barrier, inc=1, device_id=device, device_id_type=MESH)

    adj_copies = [pltpu.make_async_copy(adj_ref.at[0, 0, t], adj_in.at[t], asem.at[t]) for t in range(4)]
    own_copy = pltpu.make_async_copy(feat_ref, gath.at[row], lsem.at[0])
    cot_copy = pltpu.make_async_copy(cot_ref, cot, lsem.at[1])
    w_copy = pltpu.make_async_copy(weight_ref, w_full.at[pl.ds(rep * width, width)], lsem.at[2])
    bias_copy = pltpu.make_async_copy(bias_ref, bias, lsem.at[4])
    ints = ((rows_ref, rows_at), (cols_ref, cols), (counts_ref, counts))
    int_copies = [pltpu.make_async_copy(source, place, lsem.at[5 + k]) for k, (source, place) in enumerate(ints)]

    pl.semaphore_wait(barrier, 7)

    def slot(plane, hops, way):
        return plane * nz + (z + nz - hops if way == 0 else z + hops) % nz

    def rows_of(way, c):
        return pl.ds((c if way == 0 else 3 - c) * CHUNK, CHUNK)

    def over_z(other, hops, way, c, first=False):
        plane = 1 - x_lo if other else x_lo
        place = slot(plane, hops - 1, way)
        source = feat_ref if first else gath.at[place]
        rows = rows_of(way, c)
        return remote(
            source.at[rows],
            gath.at[place, rows],
            zs.at[other],
            zr.at[way, hops - 1, c + 2 if other else c],
            z_dev[way],
        )

    def landed_z(other, hops, way, c):
        place = gath.at[slot(1 - x_lo if other else x_lo, hops, way), rows_of(way, c)]
        remote(place, place, zs.at[0], zr.at[way, hops - 1, c + 2 if other else c], z_dev[way]).wait_recv()

    def over_x(hops, way, c):
        piece = gath.at[slot(x_lo, hops, way), rows_of(way, c)]
        return remote(piece, piece, xs.at[0], xr.at[way, hops - 1, c], x_dev)

    def landed_x(hops, way, c):
        piece = gath.at[slot(1 - x_lo, hops, way), rows_of(way, c)]
        remote(piece, piece, xs.at[0], xr.at[way, hops - 1, c], x_dev).wait_recv()

    def own_over_x(c, place):
        rows = rows_of(0, c)
        return remote(feat_ref.at[rows], gath.at[place, rows], xs.at[0], xo.at[c], x_dev)

    def over_x_count(hops):
        return 3 if hops < far - 1 else 2

    for c in (3, 0):
        own_over_x(c, row).start()
    for c in OWN_ORDER:
        for way in (0, 1):
            over_z(0, 1, way, c, True).start()
    for c in (2, 1):
        own_over_x(c, row).start()
    own_copies = (own_copy, cot_copy, w_copy, bias_copy, *int_copies)
    for copy in (*adj_copies, *own_copies):
        copy.start()
    w_send = remote(weight_ref, w_full.at[pl.ds(rep * width, width)], wsem.at[0], wsem.at[1], rep_dev)
    w_send.start()

    step = 32
    steps = block // step * 4

    def split(first, count):
        def one(i, carry):
            t, low = i // (block // step), pl.multiple_of((i % (block // step)) * step, step)
            value = adj_in[t, pl.ds(low, step), :]
            high = value.astype(BF16)
            adj_hi[t, pl.ds(low, step), :] = high
            adj_lo[t, pl.ds(low, step), :] = (value - high.astype(F32)).astype(BF16)
            return carry

        lax.fori_loop(first, first + count, one, 0)

    partner = (1 - x_lo) * nz + z
    for way, c in ((0, 3), (1, 0)):
        own_over_x(c, partner).wait_recv()
        over_z(1, 1, way, 3).start()
    done = 0
    for hops in range(1, far):
        last = hops == far - 1
        for c in OWN_ORDER:
            for way in (0, 1):
                landed_z(0, hops, way, c)
                if not last or c >= 2:
                    over_z(0, hops + 1, way, c).start()
                if c < over_x_count(hops):
                    over_x(hops, way, c).start()
        if last:
            for way in (0, 1):
                landed_x(far - 2, way, 2)
                over_z(1, far - 1, way, 2).start()
        for way in (0, 1):
            landed_z(1, hops, way, 3)
            over_z(1, hops + 1, way, 3).start()
        if hops == 1:
            for copy in adj_copies:
                copy.wait()
        upto = steps * hops // (far - 1)
        split(done, upto - done)
        done = upto
    for way in (0, 1):
        landed_z(1, far - 1, way, 2)
        over_z(1, far, way, 2).start()
    for c in (1, 2):
        own_over_x(c, partner).wait_recv()
    for hops in range(1, far):
        for c in range(over_x_count(hops)):
            for way in (0, 1):
                if (hops, c) != (far - 2, 2):
                    landed_x(hops, way, c)
    for copy in own_copies:
        copy.wait()
    for c in (2, 3):
        for way in (0, 1):
            landed_z(0, far, way, c)
    for c in (3, 2):
        for way in (0, 1):
            landed_z(1, far, way, c)

    count = counts[0, 0]
    for t in range(4):
        value = gath[jnp.clip(cols[0, 0, t], 0, 2 * nz - 1)]
        high = value.astype(BF16)
        low = (value - high.astype(F32)).astype(BF16)
        dims = (((1,), (1,)), ((), ()))
        both = lax.dot_general(jnp.concatenate([high, low], axis=0), adj_hi[t], dims, preferred_element_type=F32)
        rest = lax.dot_general(high, adj_lo[t], dims, preferred_element_type=F32)
        product = both[:width] + both[width:] + rest
        for h in (0, 1):
            prod[t, h] = product[:, h * half_b : (h + 1) * half_b]

    def placed(group, h):
        total = None
        for t in range(4):
            scale = jnp.where((t < count) & (rows_at[0, 0, t] == group), F32(1.0), F32(0.0))
            term = prod[t, h] * scale
            total = term if total is None else total + term
        return total

    order = ((0, 1 - rep), (1, rep))
    core_copies = {}
    for n, h in order:
        for k, offset in enumerate(OFFSETS):
            m_out[n, k] = placed(((y + offset) % NY) * 2 + 1 - core, h)
            copy = remote(m_out.at[n, k], c1_in.at[n, k], csem.at[0, n, k], csem.at[1, n, k], core_dev)
            copy.start()
            core_copies[n, k] = copy
    up, down = pl.ds(0, half_w), pl.ds(half_w, half_w)
    y_copies = {}

    def over_y(src, dst, name, n, way):
        index = ("relay0", "relay1", "direct0", "direct1", "final0", "final1").index(name) * 2 + n
        copy = remote(src, dst, ysend.at[index], ysem.at[index], y_dev[way])
        copy.start()
        y_copies[name, n] = copy

    for n, h in order:
        for k, offset in enumerate(OFFSETS):
            total = placed(((y + offset) % NY) * 2 + core, h)
            core_copies[n, k].wait_recv()
            s_buf[n, k] = total + c1_in[n, k]
            if offset == 2:
                over_y(s_buf.at[n, k, up], relay.at[0, n], "relay0", n, 0)
                over_y(s_buf.at[n, k, down], relay.at[1, n], "relay1", n, 1)
            elif offset == 1:
                over_y(s_buf.at[n, k, down], direct.at[1, n], "direct1", n, 0)
            elif offset == 3:
                over_y(s_buf.at[n, k, up], direct.at[0, n], "direct0", n, 1)
    for n in (0, 1):
        y_copies["relay0", n].wait_recv()
        mid[0, n] = relay[0, n] + s_buf[n, 1, up]
        over_y(mid.at[0, n], final.at[0, n], "final0", n, 0)
        y_copies["relay1", n].wait_recv()
        mid[1, n] = relay[1, n] + s_buf[n, 2, down]
        over_y(mid.at[1, n], final.at[1, n], "final1", n, 1)
    away_copy = remote(away, mt.at[pl.ds(rep * width, width)], dsem.at[0], dsem.at[1], rep_dev)
    for n in (0, 1):
        for part in (0, 1):
            y_copies["direct%d" % part, n].wait_recv()
            y_copies["final%d" % part, n].wait_recv()
            rows = pl.ds(part * half_w, half_w)
            total = s_buf[n, 3, rows] + final[part, n] + direct[part, n]
            if n == 0:
                away[rows] = total
            else:
                mt[pl.ds(pl.multiple_of(rep * width + part * half_w, half_w), half_w), :] = total
        if n == 0:
            away_copy.start()
    w_send.wait_recv()
    away_copy.wait_recv()

    preact = jnp.dot(mt[...].T, w_full[...], precision=HIGHEST, preferred_element_type=F32) + bias[...]
    squash = 1.0 / (1.0 + jnp.exp(-preact))
    out_v[...] = preact * squash
    out_copy = pltpu.make_async_copy(out_v, out_ref, lsem.at[3])
    out_copy.start()
    slope = cot[...] * squash * (1.0 + preact * (1.0 - squash))
    grad = jnp.dot(mt[...], slope, precision=HIGHEST, preferred_element_type=F32)
    for k in range(PIECES):
        g_buf[k] = grad[4 * k : 4 * k + 4]
    b_one[...] = jnp.sum(slope, axis=0, keepdims=True)

    def in_plane(peer):
        return {"row": (peer // 8 % 2) * nz + z, "col": peer % 8, "rep": peer // 16}

    me = rep * 16 + x_lo * 8 + col
    for j in range(1, PIECES):
        peer = (me + j) % PIECES
        remote(g_buf.at[peer], f1_in.at[j - 1], fsem.at[0], fsem.at[1], in_plane(peer)).start()
        remote(b_one, b1_in.at[j - 1], fsem.at[2], fsem.at[3], in_plane(peer)).start()
    own_piece, own_bias = g_buf[me], b_one[...]
    remote(f1_in, f1_in, fsem.at[0], fsem.at[1], rep_dev).wait_recv()
    remote(b1_in, b1_in, fsem.at[2], fsem.at[3], rep_dev).wait_recv()
    mine = jnp.sum(f1_in[...], axis=0) + own_piece
    bias_sum = jnp.sum(b1_in[...], axis=0) + own_bias
    p2[...] = mine
    f2_in[z] = mine
    b_two[...] = bias_sum
    b2_in[z] = bias_sum
    for k in sorted(range(1, nz), key=lambda j: -min(j, nz - j)):
        device = {"row": x_lo * nz + (z + k) % nz}
        remote(p2, f2_in.at[z], fsem.at[4], fsem.at[5], device).start()
        remote(b_two, b2_in.at[z], fsem.at[6], fsem.at[7], device).start()
    others = pl.ds(0, nz - 1)
    remote(f2_in.at[others], f2_in.at[others], fsem.at[4], fsem.at[5], rep_dev).wait_recv()
    mine = jnp.sum(f2_in[...], axis=0)
    p3[...] = mine
    here = x_lo * 8 + col
    f3_in[here] = mine
    for j in range(1, 16):
        device = in_plane(rep * 16 + (here + j) % 16)
        remote(p3, f3_in.at[here], fsem.at[8], fsem.at[9], device).start()
    remote(b2_in.at[others], b2_in.at[others], fsem.at[6], fsem.at[7], rep_dev).wait()
    gb_ref[...] = jnp.sum(b2_in[...], axis=0)
    f3_others = f3_in.at[pl.ds(0, 15)]
    remote(f3_others, f3_others, fsem.at[8], fsem.at[9], rep_dev).wait()
    for k in range(16):
        gw_ref[4 * k : 4 * k + 4, :] = f3_in[k]

    out_copy.wait()
    part = gath.at[pl.ds(0, nz - 1)]
    remote(part, part, zs.at[0], xo.at[0], rep_dev).wait_send()
    part = gath.at[pl.ds(0, far // 2 + 1)]
    remote(part, part, zs.at[1], xo.at[0], rep_dev).wait_send()
    part = gath.at[pl.ds(0, 3 * (far - 2) // 2 + 2)]
    remote(part, part, xs.at[0], xo.at[0], rep_dev).wait_send()
    w_send.wait_send()
    away_copy.wait_send()
    for copy in (*core_copies.values(), *y_copies.values()):
        copy.wait_send()
    remote(f1_in, f1_in, fsem.at[0], fsem.at[1], rep_dev).wait_send()
    remote(b1_in, b1_in, fsem.at[2], fsem.at[3], rep_dev).wait_send()
    remote(f2_in.at[others], f2_in.at[others], fsem.at[4], fsem.at[5], rep_dev).wait_send()


def solution(mesh):
    nz = mesh.shape["row"] // 2

    def local(adj_tiles, tile_rows, tile_cols, tile_counts, features_t, weight, bias_vec, cotangent):
        width, block = features_t.shape
        half_w, half_b = width // 2, block // 2
        out_w = weight.shape[1]
        nodes = cotangent.shape[0]
        vmem = pl.BlockSpec(memory_space=pltpu.VMEM)
        hbm = pl.BlockSpec(memory_space=pltpu.HBM)
        dma = pltpu.SemaphoreType.DMA
        output, grad_weight, grad_bias = pl.pallas_call(
            functools.partial(kernel, nz),
            out_shape=(
                jax.ShapeDtypeStruct((nodes, out_w), F32),
                jax.ShapeDtypeStruct((width, out_w), F32),
                jax.ShapeDtypeStruct((1, out_w), F32),
            ),
            in_specs=[hbm] * 8,
            out_specs=(hbm, vmem, vmem),
            scratch_shapes=[
                pltpu.SMEM(tile_rows.shape, jnp.int32),
                pltpu.SMEM(tile_cols.shape, jnp.int32),
                pltpu.SMEM(tile_counts.shape, jnp.int32),
                pltpu.VMEM((1, out_w), F32),
                pltpu.VMEM((2 * nz, width, block), F32),
                pltpu.VMEM((4, block, block), F32),
                pltpu.VMEM((4, block, block), BF16),
                pltpu.VMEM((4, block, block), BF16),
                pltpu.VMEM((4, 2, width, half_b), F32),
                pltpu.VMEM((2, 4, width, half_b), F32),
                pltpu.VMEM((2, 4, width, half_b), F32),
                pltpu.VMEM((2, 4, width, half_b), F32),
                pltpu.VMEM((2, 2, half_w, half_b), F32),
                pltpu.VMEM((2, 2, half_w, half_b), F32),
                pltpu.VMEM((2, 2, half_w, half_b), F32),
                pltpu.VMEM((2, 2, half_w, half_b), F32),
                pltpu.VMEM((width, half_b), F32),
                pltpu.VMEM((2 * width, half_b), F32),
                pltpu.VMEM((2 * width, out_w), F32),
                pltpu.VMEM((nodes, out_w), F32),
                pltpu.VMEM((nodes, out_w), F32),
                pltpu.VMEM((PIECES, 4, out_w), F32),
                pltpu.VMEM((PIECES - 1, 4, out_w), F32),
                pltpu.VMEM((nz, 4, out_w), F32),
                pltpu.VMEM((16, 4, out_w), F32),
                pltpu.VMEM((4, out_w), F32),
                pltpu.VMEM((4, out_w), F32),
                pltpu.VMEM((1, out_w), F32),
                pltpu.VMEM((1, out_w), F32),
                pltpu.VMEM((PIECES - 1, 1, out_w), F32),
                pltpu.VMEM((nz, 1, out_w), F32),
                dma((2, nz // 2, 6)),
                dma((2, nz // 2 - 1, 3)),
                dma((4,)),
                dma((2,)),
                dma((1,)),
                dma((8,)),
                dma((4,)),
                dma((2,)),
                dma((2, 2, 4)),
                dma((12,)),
                dma((12,)),
                dma((2,)),
                dma((12,)),
            ],
            compiler_params=pltpu.CompilerParams(
                collective_id=0, has_side_effects=True, vmem_limit_bytes=67043328
            ),
        )(tile_rows, tile_cols, tile_counts, adj_tiles, features_t, weight, bias_vec.reshape(1, out_w), cotangent)
        return output, grad_weight, grad_bias.reshape(out_w)

    return jax.shard_map(
        local,
        mesh=mesh,
        in_specs=(
            P("row", "col", None, None, None),
            P("row", "col", None),
            P("row", "col", None),
            P("row", "col"),
            P("rep", ("row", "col")),
            P("rep", None),
            P(),
            P(("row", "col", "rep"), None),
        ),
        out_specs=(P(("row", "col", "rep"), None), P("rep", None), P()),
        check_vma=False,
    )
```

```python
import functools

import jax
import jax.numpy as jnp
from jax import lax
from jax.experimental import pallas as pl
from jax.experimental.pallas import tpu as pltpu
from jax.sharding import PartitionSpec as P

MESH = pl.DeviceIdType.MESH
F32 = jnp.float32
BF16 = jnp.bfloat16
HIGHEST = lax.Precision.HIGHEST

NY = 4
PIECES = 32
CHUNK = 16
OWN_ORDER = (2, 0, 1, 3)
SENDING = ((0, 2), (0, 1), (0, 3), (1, 2), (0, 0), (1, 1), (1, 3), (1, 0))


def remote(src, dst, send_sem, recv_sem, device):
    return pltpu.make_async_remote_copy(
        src_ref=src, dst_ref=dst, send_sem=send_sem, recv_sem=recv_sem, device_id=device, device_id_type=MESH
    )


def kernel(
    nz,
    rows_ref, cols_ref, counts_ref, adj_ref, feat_ref, weight_ref, bias_ref, cot_ref,
    out_ref, gw_ref, gb_ref,
    rows_at, cols, counts, bias, gath, adj_in, adj_hi, adj_lo, prod, m_out, c1_in, s_buf,
    y_in, mt, w_full, cot, out_v,
    g_buf, f1_in, f2_in, f3_in, p2, p3,
    zr, xr, xo, zs, xs, lsem, asem, wsem, csem, ysem, fsem, ready,
):
    row, col, rep = lax.axis_index("row"), lax.axis_index("col"), lax.axis_index("rep")
    x_lo, z = row // nz, row % nz
    y, core = col // 2, col % 2
    far = nz // 2
    width, block = feat_ref.shape
    half_w, half_b = width // 2, block // 2

    z_dev = ({"row": x_lo * nz + (z + 1) % nz}, {"row": x_lo * nz + (z + nz - 1) % nz})
    x_dev = {"row": (1 - x_lo) * nz + z}
    core_dev = {"col": y * 2 + 1 - core}
    y_dev = ({"col": ((y + 1) % NY) * 2 + core}, {"col": ((y + NY - 1) % NY) * 2 + core})
    rep_dev = {"rep": 1 - rep}

    cols_of = [col] + [(col + j) % 8 for j in range(1, 8)]
    planes = []
    for i in range(4):
        x = (rep * 2 + x_lo + i) % 4
        planes.append((x // 2 * 16 + x % 2 * 8, x % 2 * nz + z, x // 2))
    z_devs = [{"row": x_lo * nz + (z + k) % nz} for k in sorted(range(1, nz), key=lambda j: -min(j, nz - j))]

    barrier = pltpu.get_barrier_semaphore()
    for device in (*z_dev, x_dev, core_dev, *y_dev, rep_dev):
        pl.semaphore_signal(barrier, inc=1, device_id=device, device_id_type=MESH)

    adj_copies = [pltpu.make_async_copy(adj_ref.at[0, 0, t], adj_in.at[t], asem.at[t]) for t in range(4)]
    own_copy = pltpu.make_async_copy(feat_ref, gath.at[row], lsem.at[0])
    cot_copy = pltpu.make_async_copy(cot_ref, cot, lsem.at[1])
    w_copy = pltpu.make_async_copy(weight_ref, w_full.at[pl.ds(rep * width, width)], lsem.at[2])
    bias_copy = pltpu.make_async_copy(bias_ref, bias, lsem.at[4])
    ints = ((rows_ref, rows_at), (cols_ref, cols), (counts_ref, counts))
    int_copies = [pltpu.make_async_copy(source, place, lsem.at[5 + k]) for k, (source, place) in enumerate(ints)]

    pl.semaphore_wait(barrier, 7)
    near = (*y_dev, rep_dev)
    for device in near:
        pl.semaphore_signal(ready.at[0], inc=1, device_id=device, device_id_type=MESH)

    def slot(plane, hops, way):
        return plane * nz + (z + nz - hops if way == 0 else z + hops) % nz

    def rows_of(way, c):
        return pl.ds((c if way == 0 else 3 - c) * CHUNK, CHUNK)

    def over_z(other, hops, way, c, first=False):
        plane = 1 - x_lo if other else x_lo
        place = slot(plane, hops - 1, way)
        source = feat_ref if first else gath.at[place]
        rows = rows_of(way, c)
        return remote(
            source.at[rows],
            gath.at[place, rows],
            zs.at[other],
            zr.at[way, hops - 1, c + 2 if other else c],
            z_dev[way],
        )

    def landed_z(other, hops, way, c):
        place = gath.at[slot(1 - x_lo if other else x_lo, hops, way), rows_of(way, c)]
        remote(place, place, zs.at[0], zr.at[way, hops - 1, c + 2 if other else c], z_dev[way]).wait_recv()

    def over_x(hops, way, c):
        piece = gath.at[slot(x_lo, hops, way), rows_of(way, c)]
        return remote(piece, piece, xs.at[0], xr.at[way, hops - 1, c], x_dev)

    def landed_x(hops, way, c):
        piece = gath.at[slot(1 - x_lo, hops, way), rows_of(way, c)]
        remote(piece, piece, xs.at[0], xr.at[way, hops - 1, c], x_dev).wait_recv()

    def own_over_x(c, place):
        rows = rows_of(0, c)
        return remote(feat_ref.at[rows], gath.at[place, rows], xs.at[0], xo.at[c], x_dev)

    def over_x_count(hops):
        return 3 if hops < far - 1 else 2

    for c in (3, 0):
        own_over_x(c, row).start()
    for c in OWN_ORDER:
        for way in (0, 1):
            over_z(0, 1, way, c, True).start()
    for c in (2, 1):
        own_over_x(c, row).start()
    own_copies = (own_copy, cot_copy, w_copy, bias_copy, *int_copies)
    for copy in (*adj_copies, *own_copies):
        copy.start()
    w_send = remote(weight_ref, w_full.at[pl.ds(rep * width, width)], wsem.at[0], wsem.at[1], rep_dev)
    w_send.start()

    step = 32
    steps = block // step * 4

    def split(first, count):
        def one(i, carry):
            t, low = i // (block // step), pl.multiple_of((i % (block // step)) * step, step)
            value = adj_in[t, pl.ds(low, step), :]
            high = value.astype(BF16)
            adj_hi[t, pl.ds(low, step), :] = high
            adj_lo[t, pl.ds(low, step), :] = (value - high.astype(F32)).astype(BF16)
            return carry

        lax.fori_loop(first, first + count, one, 0)

    partner = (1 - x_lo) * nz + z
    for way, c in ((0, 3), (1, 0)):
        own_over_x(c, partner).wait_recv()
        over_z(1, 1, way, 3).start()
    done = 0
    for hops in range(1, far):
        last = hops == far - 1
        for c in OWN_ORDER:
            for way in (0, 1):
                landed_z(0, hops, way, c)
                if not last or c >= 2:
                    over_z(0, hops + 1, way, c).start()
                if c < over_x_count(hops):
                    over_x(hops, way, c).start()
        if last:
            for way in (0, 1):
                landed_x(far - 2, way, 2)
                over_z(1, far - 1, way, 2).start()
        for way in (0, 1):
            landed_z(1, hops, way, 3)
            over_z(1, hops + 1, way, 3).start()
        if hops == 1:
            for copy in adj_copies:
                copy.wait()
        if hops == 3:
            pl.semaphore_wait(ready.at[0], 3)
            for device in near:
                pl.semaphore_signal(ready.at[1], inc=1, device_id=device, device_id_type=MESH)
        upto = steps * hops // (far - 1)
        split(done, upto - done)
        done = upto
    for way in (0, 1):
        landed_z(1, far - 1, way, 2)
        over_z(1, far, way, 2).start()
    for c in (1, 2):
        own_over_x(c, partner).wait_recv()
    for hops in range(1, far):
        for c in range(over_x_count(hops)):
            for way in (0, 1):
                if (hops, c) != (far - 2, 2):
                    landed_x(hops, way, c)
    for copy in own_copies:
        copy.wait()
    pl.semaphore_wait(ready.at[1], 3)
    for c in (2, 3):
        for way in (0, 1):
            landed_z(0, far, way, c)
    for c in (3, 2):
        for way in (0, 1):
            landed_z(1, far, way, c)

    count = counts[0, 0]
    for t in range(4):
        value = gath[jnp.clip(cols[0, 0, t], 0, 2 * nz - 1)]
        high = value.astype(BF16)
        low = (value - high.astype(F32)).astype(BF16)
        dims = (((1,), (1,)), ((), ()))
        both = lax.dot_general(jnp.concatenate([high, low], axis=0), adj_hi[t], dims, preferred_element_type=F32)
        rest = lax.dot_general(high, adj_lo[t], dims, preferred_element_type=F32)
        product = both[:width] + both[width:] + rest
        for h in (0, 1):
            prod[t, h] = product[:, h * half_b : (h + 1) * half_b]

    def placed(group, h):
        total = None
        for t in range(4):
            scale = jnp.where((t < count) & (rows_at[0, 0, t] == group), F32(1.0), F32(0.0))
            term = prod[t, h] * scale
            total = term if total is None else total + term
        return total

    order = ((0, 1 - rep), (1, rep))
    core_copies = {}
    for n, k in SENDING:
        m_out[n, k] = placed(((y + k) % NY) * 2 + 1 - core, order[n][1])
        copy = remote(m_out.at[n, k], c1_in.at[n, k], csem.at[0, n, k], csem.at[1, n, k], core_dev)
        copy.start()
        core_copies[n, k] = copy
    y_copies = {}
    for n, k in SENDING:
        total = placed(((y + k) % NY) * 2 + core, order[n][1])
        core_copies[n, k].wait_recv()
        s_buf[n, k] = total + c1_in[n, k]
        if (n, k) != (1, 0):
            device = {"col": ((y + k) % NY) * 2 + core, "rep": order[n][1]}
            copy = remote(s_buf.at[n, k], y_in.at[n, k], ysem.at[0, n, k], ysem.at[1, n, k], device)
            copy.start()
            y_copies[n, k] = copy
    for n, k in SENDING:
        if (n, k) in y_copies:
            y_copies[n, k].wait_recv()
    mt[pl.ds(pl.multiple_of(rep * width, width), width), :] = s_buf[1, 0] + y_in[1, 1] + y_in[1, 2] + y_in[1, 3]
    mt[pl.ds(pl.multiple_of((1 - rep) * width, width), width), :] = y_in[0, 0] + y_in[0, 1] + y_in[0, 2] + y_in[0, 3]
    w_send.wait_recv()

    preact = jnp.dot(mt[...].T, w_full[...], precision=HIGHEST, preferred_element_type=F32) + bias[...]
    squash = 1.0 / (1.0 + jnp.exp(-preact))
    out_v[...] = preact * squash
    out_copy = pltpu.make_async_copy(out_v, out_ref, lsem.at[3])
    out_copy.start()
    slope = cot[...] * squash * (1.0 + preact * (1.0 - squash))
    grad = jnp.dot(mt[...], slope, precision=HIGHEST, preferred_element_type=F32)
    bias_row = jnp.sum(slope, axis=0, keepdims=True)
    for k in range(PIECES):
        g_buf[k, 0:4] = grad[4 * k : 4 * k + 4]
        g_buf[k, 4:5] = bias_row

    for i in range(4):
        for j in range(8):
            if i + j > 0:
                piece, slot_at = planes[i][0] + cols_of[j], i * 8 + j - 1
                device = {"row": planes[i][1], "rep": planes[i][2], "col": cols_of[j]}
                remote(g_buf.at[piece], f1_in.at[slot_at], fsem.at[0], fsem.at[1], device).start()
    own_piece = g_buf[planes[0][0] + col]
    remote(f1_in, f1_in, fsem.at[0], fsem.at[1], rep_dev).wait_recv()
    mine = jnp.sum(f1_in[...], axis=0) + own_piece
    p2[...] = mine
    f2_in[z] = mine
    for device in z_devs:
        remote(p2, f2_in.at[z], fsem.at[2], fsem.at[3], device).start()
    others = f2_in.at[pl.ds(0, nz - 1)]
    remote(others, others, fsem.at[2], fsem.at[3], rep_dev).wait_recv()
    mine = jnp.sum(f2_in[...], axis=0)
    p3[...] = mine[0:4]
    here = x_lo * 8 + col
    f3_in[here] = mine[0:4]
    for i in (0, 1):
        for j in range(8):
            if i + j > 0:
                device = {"row": (x_lo + i - 2 * i * x_lo) * nz + z, "col": cols_of[j]}
                remote(p3, f3_in.at[here], fsem.at[4], fsem.at[5], device).start()
    gb_ref[...] = mine[4:5]
    f3_others = f3_in.at[pl.ds(0, 15)]
    remote(f3_others, f3_others, fsem.at[4], fsem.at[5], rep_dev).wait()
    for k in range(16):
        gw_ref[4 * k : 4 * k + 4, :] = f3_in[k]

    out_copy.wait()
    part = gath.at[pl.ds(0, nz - 1)]
    remote(part, part, zs.at[0], xo.at[0], rep_dev).wait_send()
    part = gath.at[pl.ds(0, far // 2 + 1)]
    remote(part, part, zs.at[1], xo.at[0], rep_dev).wait_send()
    part = gath.at[pl.ds(0, 3 * (far - 2) // 2 + 2)]
    remote(part, part, xs.at[0], xo.at[0], rep_dev).wait_send()
    w_send.wait_send()
    for copy in (*core_copies.values(), *y_copies.values()):
        copy.wait_send()
    remote(f1_in, f1_in, fsem.at[0], fsem.at[1], rep_dev).wait_send()
    remote(others, others, fsem.at[2], fsem.at[3], rep_dev).wait_send()


def hand_over(output, grad_weight, grad_bias, out_ref, gw_ref, gb_ref):
    out_ref[...] = output[...]
    gw_ref[...] = grad_weight[...]
    gb_ref[...] = grad_bias[...]


def solution(mesh):
    nz = mesh.shape["row"] // 2

    def local(adj_tiles, tile_rows, tile_cols, tile_counts, features_t, weight, bias_vec, cotangent):
        width, block = features_t.shape
        half_w, half_b = width // 2, block // 2
        out_w = weight.shape[1]
        nodes = cotangent.shape[0]
        vmem = pl.BlockSpec(memory_space=pltpu.VMEM)
        hbm = pl.BlockSpec(memory_space=pltpu.HBM)
        dma = pltpu.SemaphoreType.DMA
        output, grad_weight, grad_bias = pl.pallas_call(
            functools.partial(kernel, nz),
            out_shape=(
                jax.ShapeDtypeStruct((nodes, out_w), F32),
                jax.ShapeDtypeStruct((width, out_w), F32),
                jax.ShapeDtypeStruct((1, out_w), F32),
            ),
            in_specs=[hbm] * 8,
            out_specs=(hbm, vmem, vmem),
            scratch_shapes=[
                pltpu.SMEM(tile_rows.shape, jnp.int32),
                pltpu.SMEM(tile_cols.shape, jnp.int32),
                pltpu.SMEM(tile_counts.shape, jnp.int32),
                pltpu.VMEM((1, out_w), F32),
                pltpu.VMEM((2 * nz, width, block), F32),
                pltpu.VMEM((4, block, block), F32),
                pltpu.VMEM((4, block, block), BF16),
                pltpu.VMEM((4, block, block), BF16),
                pltpu.VMEM((4, 2, width, half_b), F32),
                pltpu.VMEM((2, 4, width, half_b), F32),
                pltpu.VMEM((2, 4, width, half_b), F32),
                pltpu.VMEM((2, 4, width, half_b), F32),
                pltpu.VMEM((2, 4, width, half_b), F32),
                pltpu.VMEM((2 * width, half_b), F32),
                pltpu.VMEM((2 * width, out_w), F32),
                pltpu.VMEM((nodes, out_w), F32),
                pltpu.VMEM((nodes, out_w), F32),
                pltpu.VMEM((PIECES, 5, out_w), F32),
                pltpu.VMEM((PIECES - 1, 5, out_w), F32),
                pltpu.VMEM((nz, 5, out_w), F32),
                pltpu.VMEM((16, 4, out_w), F32),
                pltpu.VMEM((5, out_w), F32),
                pltpu.VMEM((4, out_w), F32),
                dma((2, nz // 2, 6)),
                dma((2, nz // 2 - 1, 3)),
                dma((4,)),
                dma((2,)),
                dma((1,)),
                dma((8,)),
                dma((4,)),
                dma((2,)),
                dma((2, 2, 4)),
                dma((2, 2, 4)),
                dma((6,)),
                pltpu.SemaphoreType.REGULAR((2,)),
            ],
            compiler_params=pltpu.CompilerParams(
                collective_id=0, has_side_effects=True, vmem_limit_bytes=67043328
            ),
        )(tile_rows, tile_cols, tile_counts, adj_tiles, features_t, weight, bias_vec.reshape(1, out_w), cotangent)
        output, grad_weight, grad_bias = pl.pallas_call(
            hand_over,
            out_shape=tuple(jax.ShapeDtypeStruct(a.shape, F32) for a in (output, grad_weight, grad_bias)),
            in_specs=[vmem] * 3,
            out_specs=(vmem,) * 3,
        )(output, grad_weight, grad_bias)
        return output, grad_weight, grad_bias.reshape(out_w)

    return jax.shard_map(
        local,
        mesh=mesh,
        in_specs=(
            P("row", "col", None, None, None),
            P("row", "col", None),
            P("row", "col", None),
            P("row", "col"),
            P("rep", ("row", "col")),
            P("rep", None),
            P(),
            P(("row", "col", "rep"), None),
        ),
        out_specs=(P(("row", "col", "rep"), None), P("rep", None), P()),
        check_vma=False,
    )
```

```python
import functools

import jax
import jax.numpy as jnp
from jax import lax
from jax.experimental import pallas as pl
from jax.experimental.pallas import tpu as pltpu
from jax.sharding import PartitionSpec as P

MESH = pl.DeviceIdType.MESH
F32 = jnp.float32
BF16 = jnp.bfloat16

NY = 4
PIECES = 32
CHUNK = 16
OWN_ORDER = (2, 0, 1, 3)
X_COUNT = (3, 3, 3, 3, 3, 2, 2)
SENDING = ((0, 2), (0, 1), (0, 3), (0, 0), (1, 2), (1, 1), (1, 3), (1, 0))


def remote(src, dst, send_sem, recv_sem, device):
    return pltpu.make_async_remote_copy(
        src_ref=src, dst_ref=dst, send_sem=send_sem, recv_sem=recv_sem, device_id=device, device_id_type=MESH
    )


def halves(value):
    high = value.astype(BF16)
    return high, (value - high.astype(F32)).astype(BF16)


def kernel(
    nz,
    rows_ref, cols_ref, counts_ref, adj_ref, feat_ref, weight_ref, bias_ref, cot_ref,
    out_ref, gw_ref, gb_ref,
    rows_at, cols, counts, bias, gath, adj_in, adj_hi, adj_lo, prod, m_out, c1_in, s_buf,
    y_in, mt, w_full, w_three, x_both, cot, out_v,
    g_buf, f1_in, f2_in, f3_in, p2, p3,
    zr, xr, xo, zs, xs, lsem, asem, wsem, csem, ysem, fsem, ready,
):
    row, col, rep = lax.axis_index("row"), lax.axis_index("col"), lax.axis_index("rep")
    x_lo, z = row // nz, row % nz
    y, core = col // 2, col % 2
    far = nz // 2
    width, block = feat_ref.shape
    half_b = block // 2

    z_dev = ({"row": x_lo * nz + (z + 1) % nz}, {"row": x_lo * nz + (z + nz - 1) % nz})
    x_dev = {"row": (1 - x_lo) * nz + z}
    core_dev = {"col": y * 2 + 1 - core}
    y_dev = ({"col": ((y + 1) % NY) * 2 + core}, {"col": ((y + NY - 1) % NY) * 2 + core})
    rep_dev = {"rep": 1 - rep}

    cols_of = [col] + [(col + j) % 8 for j in range(1, 8)]
    planes = []
    for i in range(4):
        x = (rep * 2 + x_lo + i) % 4
        planes.append((x // 2 * 16 + x % 2 * 8, x % 2 * nz + z, x // 2))
    z_devs = [{"row": x_lo * nz + (z + k) % nz} for k in sorted(range(1, nz), key=lambda j: -min(j, nz - j))]

    barrier = pltpu.get_barrier_semaphore()
    for device in (*z_dev, x_dev, core_dev, *y_dev, rep_dev):
        pl.semaphore_signal(barrier, inc=1, device_id=device, device_id_type=MESH)

    adj_copies = [pltpu.make_async_copy(adj_ref.at[0, 0, t], adj_in.at[t], asem.at[t]) for t in range(4)]
    own_copy = pltpu.make_async_copy(feat_ref, gath.at[row], lsem.at[0])
    cot_copy = pltpu.make_async_copy(cot_ref, cot, lsem.at[1])
    w_copy = pltpu.make_async_copy(weight_ref, w_full.at[pl.ds(rep * width, width)], lsem.at[2])
    bias_copy = pltpu.make_async_copy(bias_ref, bias, lsem.at[4])
    ints = ((rows_ref, rows_at), (cols_ref, cols), (counts_ref, counts))
    int_copies = [pltpu.make_async_copy(source, place, lsem.at[5 + k]) for k, (source, place) in enumerate(ints)]

    pl.semaphore_wait(barrier, 7)
    near = (*y_dev, rep_dev)
    for device in near:
        pl.semaphore_signal(ready.at[0], inc=1, device_id=device, device_id_type=MESH)

    def slot(plane, hops, way):
        return plane * nz + (z + nz - hops if way == 0 else z + hops) % nz

    def rows_of(way, c):
        return pl.ds((c if way == 0 else 3 - c) * CHUNK, CHUNK)

    def over_z(other, hops, way, c, first=False):
        plane = 1 - x_lo if other else x_lo
        place = slot(plane, hops - 1, way)
        source = feat_ref if first else gath.at[place]
        rows = rows_of(way, c)
        return remote(
            source.at[rows],
            gath.at[place, rows],
            zs.at[other],
            zr.at[way, hops - 1, c + 2 if other else c],
            z_dev[way],
        )

    def landed_z(other, hops, way, c):
        place = gath.at[slot(1 - x_lo if other else x_lo, hops, way), rows_of(way, c)]
        remote(place, place, zs.at[0], zr.at[way, hops - 1, c + 2 if other else c], z_dev[way]).wait_recv()

    def over_x(hops, way, c):
        piece = gath.at[slot(x_lo, hops, way), rows_of(way, c)]
        return remote(piece, piece, xs.at[0], xr.at[way, hops - 1, c], x_dev)

    def landed_x(hops, way, c):
        piece = gath.at[slot(1 - x_lo, hops, way), rows_of(way, c)]
        remote(piece, piece, xs.at[0], xr.at[way, hops - 1, c], x_dev).wait_recv()

    def own_over_x(c, place):
        rows = rows_of(0, c)
        return remote(feat_ref.at[rows], gath.at[place, rows], xs.at[0], xo.at[c], x_dev)

    for c in (3, 0):
        own_over_x(c, row).start()
    for c in OWN_ORDER:
        for way in (0, 1):
            over_z(0, 1, way, c, True).start()
    for c in (2, 1):
        own_over_x(c, row).start()
    own_copies = (own_copy, cot_copy, bias_copy, *int_copies)
    for copy in (*adj_copies, w_copy, *own_copies):
        copy.start()
    w_send = remote(weight_ref, w_full.at[pl.ds(rep * width, width)], wsem.at[0], wsem.at[1], rep_dev)
    w_send.start()

    step = 32
    steps = block // step * 4

    def split(first, count):
        def one(i, carry):
            t, low = i // (block // step), pl.multiple_of((i % (block // step)) * step, step)
            value = adj_in[t, pl.ds(low, step), :]
            high = value.astype(BF16)
            adj_hi[t, pl.ds(low, step), :] = high
            adj_lo[t, pl.ds(low, step), :] = (value - high.astype(F32)).astype(BF16)
            return carry

        lax.fori_loop(first, first + count, one, 0)

    partner = (1 - x_lo) * nz + z
    for way, c in ((0, 3), (1, 0)):
        own_over_x(c, partner).wait_recv()
        over_z(1, 1, way, 3).start()
    done = 0
    for hops in range(1, far):
        for c in OWN_ORDER:
            for way in (0, 1):
                landed_z(0, hops, way, c)
                if hops < far - 1 or c >= 2:
                    over_z(0, hops + 1, way, c).start()
                if c < X_COUNT[hops - 1]:
                    over_x(hops, way, c).start()
        if hops > 1:
            for c in range(X_COUNT[hops - 1], X_COUNT[hops - 2]):
                for way in (0, 1):
                    landed_x(hops - 1, way, c)
                    over_z(1, hops, way, c).start()
        following = X_COUNT[hops] if hops < far - 1 else 2
        for c in (3, 2):
            for way in (0, 1):
                if c >= X_COUNT[hops - 1]:
                    landed_z(1, hops, way, c)
                    if c >= following:
                        over_z(1, hops + 1, way, c).start()
        if hops == 1:
            for copy in adj_copies:
                copy.wait()
        if hops == 3:
            pl.semaphore_wait(ready.at[0], 3)
            for device in near:
                pl.semaphore_signal(ready.at[1], inc=1, device_id=device, device_id_type=MESH)
        if hops == 5:
            w_send.wait_recv()
            w_copy.wait()
            w_high, w_low = halves(w_full[...])
            w_three[...] = jnp.concatenate([w_high, w_low, w_high], axis=0)
        upto = steps * hops // (far - 1)
        split(done, upto - done)
        done = upto
    for c in (1, 2):
        own_over_x(c, partner).wait_recv()
    for hops in range(1, far):
        for c in range(X_COUNT[hops - 1]):
            for way in (0, 1):
                if hops == far - 1 or c < X_COUNT[hops]:
                    landed_x(hops, way, c)
    for copy in own_copies:
        copy.wait()
    pl.semaphore_wait(ready.at[1], 3)
    for c in (2, 3):
        for way in (0, 1):
            landed_z(0, far, way, c)
    for c in (3, 2):
        for way in (0, 1):
            landed_z(1, far, way, c)

    count = counts[0, 0]
    order = ((0, 1 - rep), (1, rep))
    for t in range(4):
        high, low = halves(gath[jnp.clip(cols[0, 0, t], 0, 2 * nz - 1)])
        x_both[t] = jnp.concatenate([high, low], axis=0)

    def placed(group, n):
        total = None
        for t in range(4):
            scale = jnp.where((t < count) & (rows_at[0, 0, t] == group), F32(1.0), F32(0.0))
            term = prod[n, t] * scale
            total = term if total is None else total + term
        return total

    core_copies = {}
    for n, h in order:
        for t in range(4):
            nodes = pl.ds(pl.multiple_of(h * half_b, half_b), half_b)
            dims = (((1,), (1,)), ((), ()))
            both = lax.dot_general(x_both[t], adj_hi[t, nodes, :], dims, preferred_element_type=F32)
            rest = lax.dot_general(x_both[t, 0:width], adj_lo[t, nodes, :], dims, preferred_element_type=F32)
            prod[n, t] = both[:width] + both[width:] + rest
        for k in (2, 1, 3, 0):
            m_out[n, k] = placed(((y + k) % NY) * 2 + 1 - core, n)
            copy = remote(m_out.at[n, k], c1_in.at[n, k], csem.at[0, n, k], csem.at[1, n, k], core_dev)
            copy.start()
            core_copies[n, k] = copy

    y_copies = {}
    for n, k in SENDING:
        total = placed(((y + k) % NY) * 2 + core, n)
        core_copies[n, k].wait_recv()
        s_buf[n, k] = total + c1_in[n, k]
        if (n, k) != (1, 0):
            device = {"col": ((y + k) % NY) * 2 + core, "rep": order[n][1]}
            copy = remote(s_buf.at[n, k], y_in.at[n, k], ysem.at[0, n, k], ysem.at[1, n, k], device)
            copy.start()
            y_copies[n, k] = copy
    for n, k in SENDING:
        if (n, k) in y_copies:
            y_copies[n, k].wait_recv()
    mt[pl.ds(pl.multiple_of(rep * width, width), width), :] = s_buf[1, 0] + y_in[1, 1] + y_in[1, 2] + y_in[1, 3]
    mt[pl.ds(pl.multiple_of((1 - rep) * width, width), width), :] = y_in[0, 0] + y_in[0, 1] + y_in[0, 2] + y_in[0, 3]
    mixed = mt[...]
    high, low = halves(mixed.T)
    preact = jnp.dot(jnp.concatenate([high, high, low], axis=1), w_three[...], preferred_element_type=F32) + bias[...]
    squash = 1.0 / (1.0 + jnp.exp(-preact))
    out_v[...] = preact * squash
    out_copy = pltpu.make_async_copy(out_v, out_ref, lsem.at[3])
    out_copy.start()
    slope = cot[...] * squash * (1.0 + preact * (1.0 - squash))
    high, low = halves(mixed)
    s_high, s_low = halves(slope)
    grad = jnp.dot(
        jnp.concatenate([high, high, low], axis=1),
        jnp.concatenate([s_high, s_low, s_high], axis=0),
        preferred_element_type=F32,
    )
    bias_row = jnp.sum(slope, axis=0, keepdims=True)
    for k in range(PIECES):
        g_buf[k, 0:4] = grad[4 * k : 4 * k + 4]
        g_buf[k, 4:5] = bias_row

    for i in (2, 1, 3, 0):
        for j in (4, 3, 5, 2, 6, 1, 7, 0):
            if i + j > 0:
                piece, slot_at = planes[i][0] + cols_of[j], i * 8 + j - 1
                device = {"row": planes[i][1], "rep": planes[i][2], "col": cols_of[j]}
                remote(g_buf.at[piece], f1_in.at[slot_at], fsem.at[0], fsem.at[1], device).start()
    own_piece = g_buf[planes[0][0] + col]
    remote(f1_in, f1_in, fsem.at[0], fsem.at[1], rep_dev).wait_recv()
    mine = jnp.sum(f1_in[...], axis=0) + own_piece
    p2[...] = mine
    f2_in[z] = mine
    for device in z_devs:
        remote(p2, f2_in.at[z], fsem.at[2], fsem.at[3], device).start()
    others = f2_in.at[pl.ds(0, nz - 1)]
    remote(others, others, fsem.at[2], fsem.at[3], rep_dev).wait_recv()
    mine = jnp.sum(f2_in[...], axis=0)
    p3[...] = mine[0:4]
    here = x_lo * 8 + col
    f3_in[here] = mine[0:4]
    for i in (1, 0):
        for j in (4, 3, 5, 2, 6, 1, 7, 0):
            if i + j > 0:
                device = {"row": (x_lo + i - 2 * i * x_lo) * nz + z, "col": cols_of[j]}
                remote(p3, f3_in.at[here], fsem.at[4], fsem.at[5], device).start()
    gb_ref[...] = mine[4:5]
    f3_others = f3_in.at[pl.ds(0, 15)]
    remote(f3_others, f3_others, fsem.at[4], fsem.at[5], rep_dev).wait()
    for k in range(16):
        gw_ref[4 * k : 4 * k + 4, :] = f3_in[k]

    out_copy.wait()
    part = gath.at[pl.ds(0, nz - 1)]
    remote(part, part, zs.at[0], xo.at[0], rep_dev).wait_send()
    part = gath.at[pl.ds(0, sum(4 - c for c in X_COUNT) + 2), pl.ds(0, 2 * CHUNK)]
    remote(part, part, zs.at[1], xo.at[0], rep_dev).wait_send()
    part = gath.at[pl.ds(0, sum(X_COUNT) + 2), pl.ds(0, 2 * CHUNK)]
    remote(part, part, xs.at[0], xo.at[0], rep_dev).wait_send()
    w_send.wait_send()
    for copy in (*core_copies.values(), *y_copies.values()):
        copy.wait_send()
    remote(f1_in, f1_in, fsem.at[0], fsem.at[1], rep_dev).wait_send()
    remote(others, others, fsem.at[2], fsem.at[3], rep_dev).wait_send()


def hand_over(output, grad_weight, grad_bias, out_ref, gw_ref, gb_ref):
    out_ref[...] = output[...]
    gw_ref[...] = grad_weight[...]
    gb_ref[...] = grad_bias[...]


def solution(mesh):
    nz = mesh.shape["row"] // 2

    def local(adj_tiles, tile_rows, tile_cols, tile_counts, features_t, weight, bias_vec, cotangent):
        width, block = features_t.shape
        half_b = block // 2
        out_w = weight.shape[1]
        nodes = cotangent.shape[0]
        vmem = pl.BlockSpec(memory_space=pltpu.VMEM)
        hbm = pl.BlockSpec(memory_space=pltpu.HBM)
        dma = pltpu.SemaphoreType.DMA
        output, grad_weight, grad_bias = pl.pallas_call(
            functools.partial(kernel, nz),
            out_shape=(
                jax.ShapeDtypeStruct((nodes, out_w), F32),
                jax.ShapeDtypeStruct((width, out_w), F32),
                jax.ShapeDtypeStruct((1, out_w), F32),
            ),
            in_specs=[hbm] * 8,
            out_specs=(hbm, vmem, vmem),
            scratch_shapes=[
                pltpu.SMEM(tile_rows.shape, jnp.int32),
                pltpu.SMEM(tile_cols.shape, jnp.int32),
                pltpu.SMEM(tile_counts.shape, jnp.int32),
                pltpu.VMEM((1, out_w), F32),
                pltpu.VMEM((2 * nz, width, block), F32),
                pltpu.VMEM((4, block, block), F32),
                pltpu.VMEM((4, block, block), BF16),
                pltpu.VMEM((4, block, block), BF16),
                pltpu.VMEM((2, 4, width, half_b), F32),
                pltpu.VMEM((2, 4, width, half_b), F32),
                pltpu.VMEM((2, 4, width, half_b), F32),
                pltpu.VMEM((2, 4, width, half_b), F32),
                pltpu.VMEM((2, 4, width, half_b), F32),
                pltpu.VMEM((2 * width, half_b), F32),
                pltpu.VMEM((2 * width, out_w), F32),
                pltpu.VMEM((6 * width, out_w), BF16),
                pltpu.VMEM((4, 2 * width, block), BF16),
                pltpu.VMEM((nodes, out_w), F32),
                pltpu.VMEM((nodes, out_w), F32),
                pltpu.VMEM((PIECES, 5, out_w), F32),
                pltpu.VMEM((PIECES - 1, 5, out_w), F32),
                pltpu.VMEM((nz, 5, out_w), F32),
                pltpu.VMEM((16, 4, out_w), F32),
                pltpu.VMEM((5, out_w), F32),
                pltpu.VMEM((4, out_w), F32),
                dma((2, nz // 2, 6)),
                dma((2, nz // 2 - 1, 3)),
                dma((4,)),
                dma((2,)),
                dma((1,)),
                dma((8,)),
                dma((4,)),
                dma((2,)),
                dma((2, 2, 4)),
                dma((2, 2, 4)),
                dma((6,)),
                pltpu.SemaphoreType.REGULAR((2,)),
            ],
            compiler_params=pltpu.CompilerParams(
                collective_id=0, has_side_effects=True, vmem_limit_bytes=67043328
            ),
        )(tile_rows, tile_cols, tile_counts, adj_tiles, features_t, weight, bias_vec.reshape(1, out_w), cotangent)
        output, grad_weight, grad_bias = pl.pallas_call(
            hand_over,
            out_shape=tuple(jax.ShapeDtypeStruct(a.shape, F32) for a in (output, grad_weight, grad_bias)),
            in_specs=[vmem] * 3,
            out_specs=(vmem,) * 3,
        )(output, grad_weight, grad_bias)
        return output, grad_weight, grad_bias.reshape(out_w)

    return jax.shard_map(
        local,
        mesh=mesh,
        in_specs=(
            P("row", "col", None, None, None),
            P("row", "col", None),
            P("row", "col", None),
            P("row", "col"),
            P("rep", ("row", "col")),
            P("rep", None),
            P(),
            P(("row", "col", "rep"), None),
        ),
        out_specs=(P(("row", "col", "rep"), None), P("rep", None), P()),
        check_vma=False,
    )
```

```python
import functools

import jax
import jax.numpy as jnp
from jax import lax
from jax.experimental import pallas as pl
from jax.experimental.pallas import tpu as pltpu
from jax.sharding import PartitionSpec as P

MESH = pl.DeviceIdType.MESH
F32 = jnp.float32
BF16 = jnp.bfloat16

NY = 4
PIECES = 32
FAR_FIRST = (2, 1, 3, 0)
CHUNK = 16
OWN_ORDER = (2, 0, 1, 3)
X_COUNT = (3, 3, 3, 3, 3, 2, 2)
SENDING = ((0, 2), (0, 1), (0, 3), (0, 0), (1, 2), (1, 1), (1, 3), (1, 0))


def remote(src, dst, send_sem, recv_sem, device):
    return pltpu.make_async_remote_copy(
        src_ref=src, dst_ref=dst, send_sem=send_sem, recv_sem=recv_sem, device_id=device, device_id_type=MESH
    )


def halves(value):
    high = value.astype(BF16)
    return high, (value - high.astype(F32)).astype(BF16)


def kernel(
    nz,
    rows_ref, cols_ref, counts_ref, adj_ref, feat_ref, weight_ref, bias_ref, cot_ref,
    out_ref, gw_ref, gb_ref,
    rows_at, cols, counts, bias, gath, adj_in, adj_hi, adj_lo, prod, m_out, c1_in, s_buf,
    y_in, mt, w_full, w_three, x_both, cot, out_v,
    g_buf, f1_in, f2_in, p2, p3, bias_v,
    zr, xr, xo, zs, xs, lsem, asem, wsem, csem, ysem, fsem, ready,
):
    row, col, rep = lax.axis_index("row"), lax.axis_index("col"), lax.axis_index("rep")
    x_lo, z = row // nz, row % nz
    y, core = col // 2, col % 2
    far = nz // 2
    width, block = feat_ref.shape
    half_b = block // 2

    z_dev = ({"row": x_lo * nz + (z + 1) % nz}, {"row": x_lo * nz + (z + nz - 1) % nz})
    x_dev = {"row": (1 - x_lo) * nz + z}
    core_dev = {"col": y * 2 + 1 - core}
    y_dev = ({"col": ((y + 1) % NY) * 2 + core}, {"col": ((y + NY - 1) % NY) * 2 + core})
    rep_dev = {"rep": 1 - rep}

    cols_of = [col] + [(col + j) % 8 for j in range(1, 8)]
    planes = []
    for i in range(4):
        x = (rep * 2 + x_lo + i) % 4
        planes.append((x // 2 * 16 + x % 2 * 8, x % 2 * nz + z, x // 2))
    z_devs = [{"row": x_lo * nz + (z + k) % nz} for k in sorted(range(1, nz), key=lambda j: -min(j, nz - j))]

    barrier = pltpu.get_barrier_semaphore()
    for device in (*z_dev, x_dev, core_dev, *y_dev, rep_dev):
        pl.semaphore_signal(barrier, inc=1, device_id=device, device_id_type=MESH)

    adj_copies = [pltpu.make_async_copy(adj_ref.at[0, 0, t], adj_in.at[t], asem.at[t]) for t in range(4)]
    own_copy = pltpu.make_async_copy(feat_ref, gath.at[row], lsem.at[0])
    cot_copy = pltpu.make_async_copy(cot_ref, cot, lsem.at[1])
    w_copy = pltpu.make_async_copy(weight_ref, w_full.at[pl.ds(rep * width, width)], lsem.at[2])
    bias_copy = pltpu.make_async_copy(bias_ref, bias, lsem.at[4])
    ints = ((rows_ref, rows_at), (cols_ref, cols), (counts_ref, counts))
    int_copies = [pltpu.make_async_copy(source, place, lsem.at[5 + k]) for k, (source, place) in enumerate(ints)]

    pl.semaphore_wait(barrier, 7)
    near = (*y_dev, rep_dev)
    for device in near:
        pl.semaphore_signal(ready.at[0], inc=1, device_id=device, device_id_type=MESH)

    def slot(plane, hops, way):
        return plane * nz + (z + nz - hops if way == 0 else z + hops) % nz

    def rows_of(way, c):
        return pl.ds((c if way == 0 else 3 - c) * CHUNK, CHUNK)

    def over_z(other, hops, way, c, first=False):
        plane = 1 - x_lo if other else x_lo
        place = slot(plane, hops - 1, way)
        source = feat_ref if first else gath.at[place]
        rows = rows_of(way, c)
        return remote(
            source.at[rows],
            gath.at[place, rows],
            zs.at[other],
            zr.at[way, hops - 1, c + 2 if other else c],
            z_dev[way],
        )

    def landed_z(other, hops, way, c):
        place = gath.at[slot(1 - x_lo if other else x_lo, hops, way), rows_of(way, c)]
        remote(place, place, zs.at[0], zr.at[way, hops - 1, c + 2 if other else c], z_dev[way]).wait_recv()

    def over_x(hops, way, c):
        piece = gath.at[slot(x_lo, hops, way), rows_of(way, c)]
        return remote(piece, piece, xs.at[0], xr.at[way, hops - 1, c], x_dev)

    def landed_x(hops, way, c):
        piece = gath.at[slot(1 - x_lo, hops, way), rows_of(way, c)]
        remote(piece, piece, xs.at[0], xr.at[way, hops - 1, c], x_dev).wait_recv()

    def own_over_x(c, place):
        rows = rows_of(0, c)
        return remote(feat_ref.at[rows], gath.at[place, rows], xs.at[0], xo.at[c], x_dev)

    for c in (3, 0):
        own_over_x(c, row).start()
    for c in OWN_ORDER:
        for way in (0, 1):
            over_z(0, 1, way, c, True).start()
    for c in (2, 1):
        own_over_x(c, row).start()
    own_copies = (own_copy, cot_copy, bias_copy, *int_copies)
    for copy in (*adj_copies, w_copy, *own_copies):
        copy.start()
    w_send = remote(weight_ref, w_full.at[pl.ds(rep * width, width)], wsem.at[0], wsem.at[1], rep_dev)
    w_send.start()

    step = 32
    steps = block // step * 4

    def split(first, count):
        def one(i, carry):
            t, low = i // (block // step), pl.multiple_of((i % (block // step)) * step, step)
            value = adj_in[t, pl.ds(low, step), :]
            high = value.astype(BF16)
            adj_hi[t, pl.ds(low, step), :] = high
            adj_lo[t, pl.ds(low, step), :] = (value - high.astype(F32)).astype(BF16)
            return carry

        lax.fori_loop(first, first + count, one, 0)

    partner = (1 - x_lo) * nz + z
    for way, c in ((0, 3), (1, 0)):
        own_over_x(c, partner).wait_recv()
        over_z(1, 1, way, 3).start()
    done = 0
    for hops in range(1, far):
        for c in OWN_ORDER:
            for way in (0, 1):
                landed_z(0, hops, way, c)
                if hops < far - 1 or c >= 2:
                    over_z(0, hops + 1, way, c).start()
                if c < X_COUNT[hops - 1]:
                    over_x(hops, way, c).start()
        if hops > 1:
            for c in range(X_COUNT[hops - 1], X_COUNT[hops - 2]):
                for way in (0, 1):
                    landed_x(hops - 1, way, c)
                    over_z(1, hops, way, c).start()
        following = X_COUNT[hops] if hops < far - 1 else 2
        for c in (3, 2):
            for way in (0, 1):
                if c >= X_COUNT[hops - 1]:
                    landed_z(1, hops, way, c)
                    if c >= following:
                        over_z(1, hops + 1, way, c).start()
        if hops == 1:
            for copy in adj_copies:
                copy.wait()
        if hops == 3:
            pl.semaphore_wait(ready.at[0], 3)
            for device in near:
                pl.semaphore_signal(ready.at[1], inc=1, device_id=device, device_id_type=MESH)
        if hops == 5:
            w_send.wait_recv()
            w_copy.wait()
            w_high, w_low = halves(w_full[...])
            w_three[...] = jnp.concatenate([w_high, w_low, w_high], axis=0)
        upto = steps * hops // (far - 1)
        split(done, upto - done)
        done = upto
    for c in (1, 2):
        own_over_x(c, partner).wait_recv()
    for hops in range(1, far):
        for c in range(X_COUNT[hops - 1]):
            for way in (0, 1):
                if hops == far - 1 or c < X_COUNT[hops]:
                    landed_x(hops, way, c)
    for copy in own_copies:
        copy.wait()
    pl.semaphore_wait(ready.at[1], 3)
    for c in (2, 3):
        for way in (0, 1):
            landed_z(0, far, way, c)
    for c in (3, 2):
        for way in (0, 1):
            landed_z(1, far, way, c)

    count = counts[0, 0]
    order = ((0, 1 - rep), (1, rep))
    for t in range(4):
        high, low = halves(gath[jnp.clip(cols[0, 0, t], 0, 2 * nz - 1)])
        x_both[t] = jnp.concatenate([high, low], axis=0)

    def placed(side, n):
        scales = {
            k: [
                jnp.where((t < count) & (rows_at[0, 0, t] == ((y + k) % NY) * 2 + side), F32(1.0), F32(0.0))
                for t in range(4)
            ]
            for k in FAR_FIRST
        }
        for low in (0, width // 2):
            rows = pl.ds(low, width // 2)
            values = [prod[n, t, rows, :] for t in range(4)]
            for k in FAR_FIRST:
                terms = [value * scale for value, scale in zip(values, scales[k])]
                yield k, rows, low > 0, (terms[0] + terms[1]) + (terms[2] + terms[3])

    core_copies = {}
    for n, h in order:
        for t in range(4):
            nodes = pl.ds(pl.multiple_of(h * half_b, half_b), half_b)
            dims = (((1,), (1,)), ((), ()))
            both = lax.dot_general(x_both[t], adj_hi[t, nodes, :], dims, preferred_element_type=F32)
            rest = lax.dot_general(x_both[t, 0:width], adj_lo[t, nodes, :], dims, preferred_element_type=F32)
            prod[n, t] = both[:width] + both[width:] + rest
        for k, rows, whole, total in placed(1 - core, n):
            m_out[n, k, rows, :] = total
            if whole:
                copy = remote(m_out.at[n, k], c1_in.at[n, k], csem.at[0, n, k], csem.at[1, n, k], core_dev)
                copy.start()
                core_copies[n, k] = copy
        for k, rows, _, total in placed(core, n):
            s_buf[n, k, rows, :] = total

    y_copies = {}
    for n, k in SENDING:
        core_copies[n, k].wait_recv()
        s_buf[n, k] += c1_in[n, k]
        if (n, k) != (1, 0):
            device = {"col": ((y + k) % NY) * 2 + core, "rep": order[n][1]}
            copy = remote(s_buf.at[n, k], y_in.at[n, k], ysem.at[0, n, k], ysem.at[1, n, k], device)
            copy.start()
            y_copies[n, k] = copy
    for n, k in SENDING:
        if (n, k) in y_copies:
            y_copies[n, k].wait_recv()
    mt[pl.ds(pl.multiple_of(rep * width, width), width), :] = s_buf[1, 0] + y_in[1, 1] + y_in[1, 2] + y_in[1, 3]
    mt[pl.ds(pl.multiple_of((1 - rep) * width, width), width), :] = y_in[0, 0] + y_in[0, 1] + y_in[0, 2] + y_in[0, 3]
    mixed = mt[...]
    high, low = halves(mixed.T)
    preact = jnp.dot(jnp.concatenate([high, high, low], axis=1), w_three[...], preferred_element_type=F32) + bias[...]
    squash = 1.0 / (1.0 + jnp.exp(-preact))
    out_v[...] = preact * squash
    out_copy = pltpu.make_async_copy(out_v, out_ref, lsem.at[3])
    out_copy.start()
    slope = cot[...] * squash * (1.0 + preact * (1.0 - squash))
    high, low = halves(mixed)
    s_high, s_low = halves(slope)
    grad = jnp.dot(
        jnp.concatenate([high, high, low], axis=1),
        jnp.concatenate([s_high, s_low, s_high], axis=0),
        preferred_element_type=F32,
    )
    bias_row = jnp.sum(slope, axis=0, keepdims=True)
    for k in range(PIECES):
        g_buf[k, 0:4] = grad[4 * k : 4 * k + 4]
        g_buf[k, 4:5] = bias_row

    for i in (2, 1, 3, 0):
        for j in (4, 3, 5, 2, 6, 1, 7, 0):
            if i + j > 0:
                piece, slot_at = planes[i][0] + cols_of[j], i * 8 + j - 1
                device = {"row": planes[i][1], "rep": planes[i][2], "col": cols_of[j]}
                remote(g_buf.at[piece], f1_in.at[slot_at], fsem.at[0], fsem.at[1], device).start()
    own_piece = g_buf[planes[0][0] + col]
    remote(f1_in, f1_in, fsem.at[0], fsem.at[1], rep_dev).wait_recv()
    mine = jnp.sum(f1_in[...], axis=0) + own_piece
    p2[...] = mine
    f2_in[z] = mine
    for device in z_devs:
        remote(p2, f2_in.at[z], fsem.at[2], fsem.at[3], device).start()
    others = f2_in.at[pl.ds(0, nz - 1)]
    remote(others, others, fsem.at[2], fsem.at[3], rep_dev).wait_recv()
    mine = jnp.sum(f2_in[...], axis=0)
    p3[...] = mine[0:4]
    here = x_lo * 8 + col
    own_out = pltpu.make_async_copy(p3, gw_ref.at[here], lsem.at[8])
    for i in (1, 0):
        for j in (4, 3, 5, 2, 6, 1, 7, 0):
            if i + j > 0:
                device = {"row": (x_lo + i - 2 * i * x_lo) * nz + z, "col": cols_of[j]}
                remote(p3, gw_ref.at[here], fsem.at[4], fsem.at[5], device).start()
    own_out.start()
    bias_v[...] = mine[4:5]
    bias_out = pltpu.make_async_copy(bias_v, gb_ref, lsem.at[9])
    bias_out.start()
    f3_others = gw_ref.at[pl.ds(0, 15)]
    remote(f3_others, f3_others, fsem.at[4], fsem.at[5], rep_dev).wait()

    for copy in (out_copy, own_out, bias_out):
        copy.wait()
    part = gath.at[pl.ds(0, nz - 1)]
    remote(part, part, zs.at[0], xo.at[0], rep_dev).wait_send()
    part = gath.at[pl.ds(0, sum(4 - c for c in X_COUNT) + 2), pl.ds(0, 2 * CHUNK)]
    remote(part, part, zs.at[1], xo.at[0], rep_dev).wait_send()
    part = gath.at[pl.ds(0, sum(X_COUNT) + 2), pl.ds(0, 2 * CHUNK)]
    remote(part, part, xs.at[0], xo.at[0], rep_dev).wait_send()
    w_send.wait_send()
    for copy in (*core_copies.values(), *y_copies.values()):
        copy.wait_send()
    remote(f1_in, f1_in, fsem.at[0], fsem.at[1], rep_dev).wait_send()
    remote(others, others, fsem.at[2], fsem.at[3], rep_dev).wait_send()


def hand_over(output, grad_weight, grad_bias, out_ref, gw_ref, gb_ref):
    out_ref[...] = output[...]
    for k in range(16):
        gw_ref[4 * k : 4 * k + 4, :] = grad_weight[k]
    gb_ref[...] = grad_bias[...]


def solution(mesh):
    nz = mesh.shape["row"] // 2

    def local(adj_tiles, tile_rows, tile_cols, tile_counts, features_t, weight, bias_vec, cotangent):
        width, block = features_t.shape
        half_b = block // 2
        out_w = weight.shape[1]
        nodes = cotangent.shape[0]
        vmem = pl.BlockSpec(memory_space=pltpu.VMEM)
        hbm = pl.BlockSpec(memory_space=pltpu.HBM)
        dma = pltpu.SemaphoreType.DMA
        output, grad_weight, grad_bias = pl.pallas_call(
            functools.partial(kernel, nz),
            out_shape=(
                jax.ShapeDtypeStruct((nodes, out_w), F32),
                jax.ShapeDtypeStruct((16, width // 16, out_w), F32),
                jax.ShapeDtypeStruct((1, out_w), F32),
            ),
            in_specs=[hbm] * 8,
            out_specs=(hbm,) * 3,
            scratch_shapes=[
                pltpu.SMEM(tile_rows.shape, jnp.int32),
                pltpu.SMEM(tile_cols.shape, jnp.int32),
                pltpu.SMEM(tile_counts.shape, jnp.int32),
                pltpu.VMEM((1, out_w), F32),
                pltpu.VMEM((2 * nz, width, block), F32),
                pltpu.VMEM((4, block, block), F32),
                pltpu.VMEM((4, block, block), BF16),
                pltpu.VMEM((4, block, block), BF16),
                pltpu.VMEM((2, 4, width, half_b), F32),
                pltpu.VMEM((2, 4, width, half_b), F32),
                pltpu.VMEM((2, 4, width, half_b), F32),
                pltpu.VMEM((2, 4, width, half_b), F32),
                pltpu.VMEM((2, 4, width, half_b), F32),
                pltpu.VMEM((2 * width, half_b), F32),
                pltpu.VMEM((2 * width, out_w), F32),
                pltpu.VMEM((6 * width, out_w), BF16),
                pltpu.VMEM((4, 2 * width, block), BF16),
                pltpu.VMEM((nodes, out_w), F32),
                pltpu.VMEM((nodes, out_w), F32),
                pltpu.VMEM((PIECES, 5, out_w), F32),
                pltpu.VMEM((PIECES - 1, 5, out_w), F32),
                pltpu.VMEM((nz, 5, out_w), F32),
                pltpu.VMEM((5, out_w), F32),
                pltpu.VMEM((4, out_w), F32),
                pltpu.VMEM((1, out_w), F32),
                dma((2, nz // 2, 6)),
                dma((2, nz // 2 - 1, 3)),
                dma((4,)),
                dma((2,)),
                dma((1,)),
                dma((10,)),
                dma((4,)),
                dma((2,)),
                dma((2, 2, 4)),
                dma((2, 2, 4)),
                dma((6,)),
                pltpu.SemaphoreType.REGULAR((2,)),
            ],
            compiler_params=pltpu.CompilerParams(
                collective_id=0, has_side_effects=True, vmem_limit_bytes=67043328
            ),
        )(tile_rows, tile_cols, tile_counts, adj_tiles, features_t, weight, bias_vec.reshape(1, out_w), cotangent)
        output, grad_weight, grad_bias = pl.pallas_call(
            hand_over,
            out_shape=tuple(
                jax.ShapeDtypeStruct(shape, F32) for shape in (output.shape, (width, out_w), grad_bias.shape)
            ),
            in_specs=[vmem] * 3,
            out_specs=(vmem,) * 3,
        )(output, grad_weight, grad_bias)
        return output, grad_weight, grad_bias.reshape(out_w)

    return jax.shard_map(
        local,
        mesh=mesh,
        in_specs=(
            P("row", "col", None, None, None),
            P("row", "col", None),
            P("row", "col", None),
            P("row", "col"),
            P("rep", ("row", "col")),
            P("rep", None),
            P(),
            P(("row", "col", "rep"), None),
        ),
        out_specs=(P(("row", "col", "rep"), None), P("rep", None), P()),
        check_vma=False,
    )
```

```python
import functools

import jax
import jax.numpy as jnp
from jax import lax
from jax.experimental import pallas as pl
from jax.experimental.pallas import tpu as pltpu
from jax.sharding import PartitionSpec as P

MESH = pl.DeviceIdType.MESH
F32 = jnp.float32
BF16 = jnp.bfloat16

NY = 4
PIECES = 32
FAR_FIRST = (2, 1, 3, 0)
CHUNK = 16
OWN_ORDER = (2, 0, 1, 3)
X_COUNT = (3, 3, 3, 3, 3, 2, 2)
SENDING = ((0, 2), (0, 1), (0, 3), (1, 2), (0, 0), (1, 1), (1, 3), (1, 0))


def remote(src, dst, send_sem, recv_sem, device):
    return pltpu.make_async_remote_copy(
        src_ref=src, dst_ref=dst, send_sem=send_sem, recv_sem=recv_sem, device_id=device, device_id_type=MESH
    )


def halves(value):
    high = value.astype(BF16)
    return high, (value - high.astype(F32)).astype(BF16)


def kernel(
    nz,
    rows_ref, cols_ref, counts_ref, adj_ref, feat_ref, weight_ref, bias_ref, cot_ref,
    out_ref, gw_ref, gb_ref,
    rows_at, cols, counts, bias, gath, adj_in, adj_hi, adj_lo, prod, m_out, c1_in, s_buf,
    y_in, mt, w_full, w_three, x_both, cot, out_v,
    g_buf, f1_in, f2_in, p2, p3, bias_v,
    zr, xr, xo, zs, xs, lsem, asem, wsem, csem, ysem, fsem, ready,
):
    row, col, rep = lax.axis_index("row"), lax.axis_index("col"), lax.axis_index("rep")
    x_lo, z = row // nz, row % nz
    y, core = col // 2, col % 2
    far = nz // 2
    width, block = feat_ref.shape
    half_b = block // 2

    z_dev = ({"row": x_lo * nz + (z + 1) % nz}, {"row": x_lo * nz + (z + nz - 1) % nz})
    x_dev = {"row": (1 - x_lo) * nz + z}
    core_dev = {"col": y * 2 + 1 - core}
    y_dev = ({"col": ((y + 1) % NY) * 2 + core}, {"col": ((y + NY - 1) % NY) * 2 + core})
    rep_dev = {"rep": 1 - rep}

    cols_of = [col] + [(col + j) % 8 for j in range(1, 8)]
    planes = []
    for i in range(4):
        x = (rep * 2 + x_lo + i) % 4
        planes.append((x // 2 * 16 + x % 2 * 8, x % 2 * nz + z, x // 2))
    z_devs = [{"row": x_lo * nz + (z + k) % nz} for k in sorted(range(1, nz), key=lambda j: -min(j, nz - j))]

    barrier = pltpu.get_barrier_semaphore()
    for device in (*z_dev, x_dev, core_dev, *y_dev, rep_dev):
        pl.semaphore_signal(barrier, inc=1, device_id=device, device_id_type=MESH)

    adj_copies = [pltpu.make_async_copy(adj_ref.at[0, 0, t], adj_in.at[t], asem.at[t]) for t in range(4)]
    own_copy = pltpu.make_async_copy(feat_ref, gath.at[row], lsem.at[0])
    cot_copy = pltpu.make_async_copy(cot_ref, cot, lsem.at[1])
    w_copy = pltpu.make_async_copy(weight_ref, w_full.at[pl.ds(rep * width, width)], lsem.at[2])
    bias_copy = pltpu.make_async_copy(bias_ref, bias, lsem.at[4])
    ints = ((rows_ref, rows_at), (cols_ref, cols), (counts_ref, counts))
    int_copies = [pltpu.make_async_copy(source, place, lsem.at[5 + k]) for k, (source, place) in enumerate(ints)]

    pl.semaphore_wait(barrier, 7)
    near = (*y_dev, rep_dev)
    for device in near:
        pl.semaphore_signal(ready.at[0], inc=1, device_id=device, device_id_type=MESH)

    def slot(plane, hops, way):
        return plane * nz + (z + nz - hops if way == 0 else z + hops) % nz

    def rows_of(way, c):
        return pl.ds((c if way == 0 else 3 - c) * CHUNK, CHUNK)

    def over_z(other, hops, way, c, first=False):
        plane = 1 - x_lo if other else x_lo
        place = slot(plane, hops - 1, way)
        source = feat_ref if first else gath.at[place]
        rows = rows_of(way, c)
        return remote(
            source.at[rows],
            gath.at[place, rows],
            zs.at[other],
            zr.at[way, hops - 1, c + 2 if other else c],
            z_dev[way],
        )

    def landed_z(other, hops, way, c):
        place = gath.at[slot(1 - x_lo if other else x_lo, hops, way), rows_of(way, c)]
        remote(place, place, zs.at[0], zr.at[way, hops - 1, c + 2 if other else c], z_dev[way]).wait_recv()

    def over_x(hops, way, c):
        piece = gath.at[slot(x_lo, hops, way), rows_of(way, c)]
        return remote(piece, piece, xs.at[0], xr.at[way, hops - 1, c], x_dev)

    def landed_x(hops, way, c):
        piece = gath.at[slot(1 - x_lo, hops, way), rows_of(way, c)]
        remote(piece, piece, xs.at[0], xr.at[way, hops - 1, c], x_dev).wait_recv()

    def own_over_x(c, place):
        rows = rows_of(0, c)
        return remote(feat_ref.at[rows], gath.at[place, rows], xs.at[0], xo.at[c], x_dev)

    for c in (3, 0):
        own_over_x(c, row).start()
    for c in OWN_ORDER:
        for way in (0, 1):
            over_z(0, 1, way, c, True).start()
    for c in (2, 1):
        own_over_x(c, row).start()
    own_copies = (own_copy, cot_copy, bias_copy, *int_copies)
    for copy in (*adj_copies, w_copy, *own_copies):
        copy.start()
    w_send = remote(weight_ref, w_full.at[pl.ds(rep * width, width)], wsem.at[0], wsem.at[1], rep_dev)
    w_send.start()

    step = 32
    steps = block // step * 4

    def split(first, count):
        def one(i, carry):
            t, low = i // (block // step), pl.multiple_of((i % (block // step)) * step, step)
            value = adj_in[t, pl.ds(low, step), :]
            high = value.astype(BF16)
            adj_hi[t, pl.ds(low, step), :] = high
            adj_lo[t, pl.ds(low, step), :] = (value - high.astype(F32)).astype(BF16)
            return carry

        lax.fori_loop(first, first + count, one, 0)

    partner = (1 - x_lo) * nz + z
    for way, c in ((0, 3), (1, 0)):
        own_over_x(c, partner).wait_recv()
        over_z(1, 1, way, 3).start()
    done = 0
    for hops in range(1, far):
        for c in OWN_ORDER:
            for way in (0, 1):
                landed_z(0, hops, way, c)
                if hops < far - 1 or c >= 2:
                    over_z(0, hops + 1, way, c).start()
                if c < X_COUNT[hops - 1]:
                    over_x(hops, way, c).start()
        if hops > 1:
            for c in range(X_COUNT[hops - 1], X_COUNT[hops - 2]):
                for way in (0, 1):
                    landed_x(hops - 1, way, c)
                    over_z(1, hops, way, c).start()
        following = X_COUNT[hops] if hops < far - 1 else 2
        for c in (3, 2):
            for way in (0, 1):
                if c >= X_COUNT[hops - 1]:
                    landed_z(1, hops, way, c)
                    if c >= following:
                        over_z(1, hops + 1, way, c).start()
        if hops == 1:
            for copy in adj_copies:
                copy.wait()
        if hops == 3:
            pl.semaphore_wait(ready.at[0], 3)
            for device in near:
                pl.semaphore_signal(ready.at[1], inc=1, device_id=device, device_id_type=MESH)
        if hops == 5:
            w_send.wait_recv()
            w_copy.wait()
            w_high, w_low = halves(w_full[...])
            w_three[...] = jnp.concatenate([w_high, w_low, w_high], axis=0)
        upto = steps * hops // (far - 1)
        split(done, upto - done)
        done = upto
    for c in (1, 2):
        own_over_x(c, partner).wait_recv()
    for hops in range(1, far):
        for c in range(X_COUNT[hops - 1]):
            for way in (0, 1):
                if hops == far - 1 or c < X_COUNT[hops]:
                    landed_x(hops, way, c)
    for copy in own_copies:
        copy.wait()
    pl.semaphore_wait(ready.at[1], 3)
    for c in (2, 3):
        for way in (0, 1):
            landed_z(0, far, way, c)
    for c in (3, 2):
        for way in (0, 1):
            landed_z(1, far, way, c)

    count = counts[0, 0]
    order = ((0, 1 - rep), (1, rep))
    for t in range(4):
        high, low = halves(gath[jnp.clip(cols[0, 0, t], 0, 2 * nz - 1)])
        x_both[t] = jnp.concatenate([high, low], axis=0)

    def placed(side, n):
        scales = {
            k: [
                jnp.where((t < count) & (rows_at[0, 0, t] == ((y + k) % NY) * 2 + side), F32(1.0), F32(0.0))
                for t in range(4)
            ]
            for k in FAR_FIRST
        }
        for low in (0, width // 2):
            rows = pl.ds(low, width // 2)
            values = [prod[n, t, rows, :] for t in range(4)]
            for k in FAR_FIRST:
                terms = [value * scale for value, scale in zip(values, scales[k])]
                yield k, rows, low > 0, (terms[0] + terms[1]) + (terms[2] + terms[3])

    core_copies = {}
    for n, h in order:
        for t in range(4):
            nodes = pl.ds(pl.multiple_of(h * half_b, half_b), half_b)
            dims = (((1,), (1,)), ((), ()))
            both = lax.dot_general(x_both[t], adj_hi[t, nodes, :], dims, preferred_element_type=F32)
            rest = lax.dot_general(x_both[t, 0:width], adj_lo[t, nodes, :], dims, preferred_element_type=F32)
            prod[n, t] = both[:width] + both[width:] + rest
        for k, rows, whole, total in placed(1 - core, n):
            m_out[n, k, rows, :] = total
            if whole:
                copy = remote(m_out.at[n, k], c1_in.at[n, k], csem.at[0, n, k], csem.at[1, n, k], core_dev)
                copy.start()
                core_copies[n, k] = copy
        for k, rows, _, total in placed(core, n):
            s_buf[n, k, rows, :] = total

    y_copies = {}
    for n, k in SENDING:
        core_copies[n, k].wait_recv()
        s_buf[n, k] += c1_in[n, k]
        if (n, k) != (1, 0):
            device = {"col": ((y + k) % NY) * 2 + core, "rep": order[n][1]}
            copy = remote(s_buf.at[n, k], y_in.at[n, k], ysem.at[0, n, k], ysem.at[1, n, k], device)
            copy.start()
            y_copies[n, k] = copy
    for n, k in SENDING:
        if (n, k) in y_copies:
            y_copies[n, k].wait_recv()
    mt[pl.ds(pl.multiple_of(rep * width, width), width), :] = s_buf[1, 0] + y_in[1, 1] + y_in[1, 2] + y_in[1, 3]
    mt[pl.ds(pl.multiple_of((1 - rep) * width, width), width), :] = y_in[0, 0] + y_in[0, 1] + y_in[0, 2] + y_in[0, 3]
    mixed = mt[...]
    high, low = halves(mixed.T)
    preact = jnp.dot(jnp.concatenate([high, high, low], axis=1), w_three[...], preferred_element_type=F32) + bias[...]
    squash = 1.0 / (1.0 + jnp.exp(-preact))
    out_v[...] = preact * squash
    out_copy = pltpu.make_async_copy(out_v, out_ref, lsem.at[3])
    out_copy.start()
    slope = cot[...] * squash * (1.0 + preact * (1.0 - squash))
    high, low = halves(mixed)
    s_high, s_low = halves(slope)
    grad = jnp.dot(
        jnp.concatenate([high, high, low], axis=1),
        jnp.concatenate([s_high, s_low, s_high], axis=0),
        preferred_element_type=F32,
    )
    bias_row = jnp.sum(slope, axis=0, keepdims=True)
    for k in range(PIECES):
        g_buf[k, 0:4] = grad[4 * k : 4 * k + 4]
        g_buf[k, 4:5] = bias_row

    for i in (2, 1, 3, 0):
        for j in (4, 3, 5, 2, 6, 1, 7, 0):
            if i + j > 0:
                piece, slot_at = planes[i][0] + cols_of[j], i * 8 + j - 1
                device = {"row": planes[i][1], "rep": planes[i][2], "col": cols_of[j]}
                remote(g_buf.at[piece], f1_in.at[slot_at], fsem.at[0], fsem.at[1], device).start()
    own_piece = g_buf[planes[0][0] + col]
    remote(f1_in, f1_in, fsem.at[0], fsem.at[1], rep_dev).wait_recv()
    mine = jnp.sum(f1_in[...], axis=0) + own_piece
    p2[...] = mine
    f2_in[z] = mine
    for device in z_devs:
        remote(p2, f2_in.at[z], fsem.at[2], fsem.at[3], device).start()
    others = f2_in.at[pl.ds(0, nz - 1)]
    remote(others, others, fsem.at[2], fsem.at[3], rep_dev).wait_recv()
    mine = jnp.sum(f2_in[...], axis=0)
    p3[...] = mine[0:4]
    here = x_lo * 8 + col
    own_out = pltpu.make_async_copy(p3, gw_ref.at[here], lsem.at[8])
    for i in (1, 0):
        for j in (4, 3, 5, 2, 6, 1, 7, 0):
            if i + j > 0:
                device = {"row": (x_lo + i - 2 * i * x_lo) * nz + z, "col": cols_of[j]}
                remote(p3, gw_ref.at[here], fsem.at[4], fsem.at[5], device).start()
    own_out.start()
    bias_v[...] = mine[4:5]
    bias_out = pltpu.make_async_copy(bias_v, gb_ref, lsem.at[9])
    bias_out.start()
    f3_others = gw_ref.at[pl.ds(0, 15)]
    remote(f3_others, f3_others, fsem.at[4], fsem.at[5], rep_dev).wait()

    for copy in (out_copy, own_out, bias_out):
        copy.wait()
    part = gath.at[pl.ds(0, nz - 1)]
    remote(part, part, zs.at[0], xo.at[0], rep_dev).wait_send()
    part = gath.at[pl.ds(0, sum(4 - c for c in X_COUNT) + 2), pl.ds(0, 2 * CHUNK)]
    remote(part, part, zs.at[1], xo.at[0], rep_dev).wait_send()
    part = gath.at[pl.ds(0, sum(X_COUNT) + 2), pl.ds(0, 2 * CHUNK)]
    remote(part, part, xs.at[0], xo.at[0], rep_dev).wait_send()
    w_send.wait_send()
    for copy in (*core_copies.values(), *y_copies.values()):
        copy.wait_send()
    remote(f1_in, f1_in, fsem.at[0], fsem.at[1], rep_dev).wait_send()
    remote(others, others, fsem.at[2], fsem.at[3], rep_dev).wait_send()


def hand_over(output, grad_weight, grad_bias, out_ref, gw_ref, gb_ref, out_v, gw_in, gw_v, gb_v, sems):
    pairs = ((grad_weight, gw_in), (output, out_v), (grad_bias, gb_v))
    copies = [pltpu.make_async_copy(source, place, sems.at[0, k]) for k, (source, place) in enumerate(pairs)]
    pairs = ((gw_v, gw_ref), (out_v, out_ref), (gb_v, gb_ref))
    stores = [pltpu.make_async_copy(source, place, sems.at[1, k]) for k, (source, place) in enumerate(pairs)]
    for copy in copies:
        copy.start()
    for k in (1, 2):
        copies[k].wait()
        stores[k].start()
    copies[0].wait()
    for k in range(16):
        gw_v[4 * k : 4 * k + 4, :] = gw_in[k]
    stores[0].start()
    for store in stores:
        store.wait()


def solution(mesh):
    nz = mesh.shape["row"] // 2

    def local(adj_tiles, tile_rows, tile_cols, tile_counts, features_t, weight, bias_vec, cotangent):
        width, block = features_t.shape
        half_b = block // 2
        out_w = weight.shape[1]
        nodes = cotangent.shape[0]
        hbm = pl.BlockSpec(memory_space=pltpu.HBM)
        dma = pltpu.SemaphoreType.DMA
        output, grad_weight, grad_bias = pl.pallas_call(
            functools.partial(kernel, nz),
            out_shape=(
                jax.ShapeDtypeStruct((nodes, out_w), F32),
                jax.ShapeDtypeStruct((16, width // 16, out_w), F32),
                jax.ShapeDtypeStruct((1, out_w), F32),
            ),
            in_specs=[hbm] * 8,
            out_specs=(hbm,) * 3,
            scratch_shapes=[
                pltpu.SMEM(tile_rows.shape, jnp.int32),
                pltpu.SMEM(tile_cols.shape, jnp.int32),
                pltpu.SMEM(tile_counts.shape, jnp.int32),
                pltpu.VMEM((1, out_w), F32),
                pltpu.VMEM((2 * nz, width, block), F32),
                pltpu.VMEM((4, block, block), F32),
                pltpu.VMEM((4, block, block), BF16),
                pltpu.VMEM((4, block, block), BF16),
                pltpu.VMEM((2, 4, width, half_b), F32),
                pltpu.VMEM((2, 4, width, half_b), F32),
                pltpu.VMEM((2, 4, width, half_b), F32),
                pltpu.VMEM((2, 4, width, half_b), F32),
                pltpu.VMEM((2, 4, width, half_b), F32),
                pltpu.VMEM((2 * width, half_b), F32),
                pltpu.VMEM((2 * width, out_w), F32),
                pltpu.VMEM((6 * width, out_w), BF16),
                pltpu.VMEM((4, 2 * width, block), BF16),
                pltpu.VMEM((nodes, out_w), F32),
                pltpu.VMEM((nodes, out_w), F32),
                pltpu.VMEM((PIECES, 5, out_w), F32),
                pltpu.VMEM((PIECES - 1, 5, out_w), F32),
                pltpu.VMEM((nz, 5, out_w), F32),
                pltpu.VMEM((5, out_w), F32),
                pltpu.VMEM((4, out_w), F32),
                pltpu.VMEM((1, out_w), F32),
                dma((2, nz // 2, 6)),
                dma((2, nz // 2 - 1, 3)),
                dma((4,)),
                dma((2,)),
                dma((1,)),
                dma((10,)),
                dma((4,)),
                dma((2,)),
                dma((2, 2, 4)),
                dma((2, 2, 4)),
                dma((6,)),
                pltpu.SemaphoreType.REGULAR((2,)),
            ],
            compiler_params=pltpu.CompilerParams(
                collective_id=0, has_side_effects=True, vmem_limit_bytes=67043328
            ),
        )(tile_rows, tile_cols, tile_counts, adj_tiles, features_t, weight, bias_vec.reshape(1, out_w), cotangent)
        output, grad_weight, grad_bias = pl.pallas_call(
            hand_over,
            out_shape=tuple(
                jax.ShapeDtypeStruct(shape, F32) for shape in (output.shape, (width, out_w), grad_bias.shape)
            ),
            in_specs=[hbm] * 3,
            out_specs=(hbm,) * 3,
            scratch_shapes=[
                pltpu.VMEM(output.shape, F32),
                pltpu.VMEM(grad_weight.shape, F32),
                pltpu.VMEM((width, out_w), F32),
                pltpu.VMEM(grad_bias.shape, F32),
                dma((2, 3)),
            ],
            compiler_params=pltpu.CompilerParams(vmem_limit_bytes=67043328),
        )(output, grad_weight, grad_bias)
        return output, grad_weight, grad_bias.reshape(out_w)

    return jax.shard_map(
        local,
        mesh=mesh,
        in_specs=(
            P("row", "col", None, None, None),
            P("row", "col", None),
            P("row", "col", None),
            P("row", "col"),
            P("rep", ("row", "col")),
            P("rep", None),
            P(),
            P(("row", "col", "rep"), None),
        ),
        out_specs=(P(("row", "col", "rep"), None), P("rep", None), P()),
        check_vma=False,
    )
```

```python
import functools

import jax
import jax.numpy as jnp
from jax import lax
from jax.experimental import pallas as pl
from jax.experimental.pallas import tpu as pltpu
from jax.sharding import PartitionSpec as P

MESH = pl.DeviceIdType.MESH
F32 = jnp.float32
BF16 = jnp.bfloat16

NY = 4
PIECES = 32
FAR_FIRST = (2, 1, 3, 0)
CHUNK = 16
OWN_ORDER = (2, 0, 1, 3)
X_COUNT = (3, 3, 3, 3, 3, 2, 2)
SENDING = ((0, 2), (0, 1), (0, 3), (0, 0), (1, 2), (1, 1), (1, 3), (1, 0))


def remote(src, dst, send_sem, recv_sem, device):
    return pltpu.make_async_remote_copy(
        src_ref=src, dst_ref=dst, send_sem=send_sem, recv_sem=recv_sem, device_id=device, device_id_type=MESH
    )


def halves(value):
    high = value.astype(BF16)
    return high, (value - high.astype(F32)).astype(BF16)


def kernel(
    nz,
    rows_ref, cols_ref, counts_ref, adj_ref, feat_ref, weight_ref, bias_ref, cot_ref,
    out_ref, gw_ref, gb_ref,
    rows_at, cols, counts, bias, gath, adj_in, adj_hi, adj_lo, prod, m_out, c1_in, s_buf,
    y_in, mt, w_full, w_three, x_both, cot, out_v,
    g_buf, f1_in, f2_in, p2, p3, bias_v,
    zr, xr, xo, zs, xs, lsem, asem, wsem, csem, ysem, fsem, ready,
):
    row, col, rep = lax.axis_index("row"), lax.axis_index("col"), lax.axis_index("rep")
    x_lo, z = row // nz, row % nz
    y, core = col // 2, col % 2
    far = nz // 2
    width, block = feat_ref.shape
    half_b = block // 2

    z_dev = ({"row": x_lo * nz + (z + 1) % nz}, {"row": x_lo * nz + (z + nz - 1) % nz})
    x_dev = {"row": (1 - x_lo) * nz + z}
    core_dev = {"col": y * 2 + 1 - core}
    y_dev = ({"col": ((y + 1) % NY) * 2 + core}, {"col": ((y + NY - 1) % NY) * 2 + core})
    rep_dev = {"rep": 1 - rep}

    cols_of = [col] + [(col + j) % 8 for j in range(1, 8)]
    planes = []
    for i in range(4):
        x = (rep * 2 + x_lo + i) % 4
        planes.append((x // 2 * 16 + x % 2 * 8, x % 2 * nz + z, x // 2))
    z_devs = [{"row": x_lo * nz + (z + k) % nz} for k in sorted(range(1, nz), key=lambda j: -min(j, nz - j))]

    barrier = pltpu.get_barrier_semaphore()
    for device in (*z_dev, x_dev, core_dev, *y_dev, rep_dev):
        pl.semaphore_signal(barrier, inc=1, device_id=device, device_id_type=MESH)

    adj_copies = [pltpu.make_async_copy(adj_ref.at[0, 0, t], adj_in.at[t], asem.at[t]) for t in range(4)]
    own_copy = pltpu.make_async_copy(feat_ref, gath.at[row], lsem.at[0])
    cot_copy = pltpu.make_async_copy(cot_ref, cot, lsem.at[1])
    w_copy = pltpu.make_async_copy(weight_ref, w_full.at[pl.ds(rep * width, width)], lsem.at[2])
    bias_copy = pltpu.make_async_copy(bias_ref, bias, lsem.at[4])
    ints = ((rows_ref, rows_at), (cols_ref, cols), (counts_ref, counts))
    int_copies = [pltpu.make_async_copy(source, place, lsem.at[5 + k]) for k, (source, place) in enumerate(ints)]

    pl.semaphore_wait(barrier, 7)
    near = (*y_dev, rep_dev)
    for device in near:
        pl.semaphore_signal(ready.at[0], inc=1, device_id=device, device_id_type=MESH)

    def slot(plane, hops, way):
        return plane * nz + (z + nz - hops if way == 0 else z + hops) % nz

    def rows_of(way, c):
        return pl.ds((c if way == 0 else 3 - c) * CHUNK, CHUNK)

    def over_z(other, hops, way, c, first=False):
        plane = 1 - x_lo if other else x_lo
        place = slot(plane, hops - 1, way)
        source = feat_ref if first else gath.at[place]
        rows = rows_of(way, c)
        return remote(
            source.at[rows],
            gath.at[place, rows],
            zs.at[other],
            zr.at[way, hops - 1, c + 2 if other else c],
            z_dev[way],
        )

    def landed_z(other, hops, way, c):
        place = gath.at[slot(1 - x_lo if other else x_lo, hops, way), rows_of(way, c)]
        remote(place, place, zs.at[0], zr.at[way, hops - 1, c + 2 if other else c], z_dev[way]).wait_recv()

    def over_x(hops, way, c):
        piece = gath.at[slot(x_lo, hops, way), rows_of(way, c)]
        return remote(piece, piece, xs.at[0], xr.at[way, hops - 1, c], x_dev)

    def landed_x(hops, way, c):
        piece = gath.at[slot(1 - x_lo, hops, way), rows_of(way, c)]
        remote(piece, piece, xs.at[0], xr.at[way, hops - 1, c], x_dev).wait_recv()

    def own_over_x(c, place):
        rows = rows_of(0, c)
        return remote(feat_ref.at[rows], gath.at[place, rows], xs.at[0], xo.at[c], x_dev)

    for c in (3, 0):
        own_over_x(c, row).start()
    for c in OWN_ORDER:
        for way in (0, 1):
            over_z(0, 1, way, c, True).start()
    for c in (2, 1):
        own_over_x(c, row).start()
    own_copies = (own_copy, cot_copy, bias_copy, *int_copies)
    for copy in (*adj_copies, w_copy, *own_copies):
        copy.start()
    w_send = remote(weight_ref, w_full.at[pl.ds(rep * width, width)], wsem.at[0], wsem.at[1], rep_dev)
    w_send.start()

    step = 32
    steps = block // step * 4

    def split(first, count):
        def one(i, carry):
            t, low = i // (block // step), pl.multiple_of((i % (block // step)) * step, step)
            value = adj_in[t, pl.ds(low, step), :]
            high = value.astype(BF16)
            adj_hi[t, pl.ds(low, step), :] = high
            adj_lo[t, pl.ds(low, step), :] = (value - high.astype(F32)).astype(BF16)
            return carry

        lax.fori_loop(first, first + count, one, 0)

    partner = (1 - x_lo) * nz + z
    for way, c in ((0, 3), (1, 0)):
        own_over_x(c, partner).wait_recv()
        over_z(1, 1, way, 3).start()
    done = 0
    for hops in range(1, far):
        for c in OWN_ORDER:
            for way in (0, 1):
                landed_z(0, hops, way, c)
                if hops < far - 1 or c >= 2:
                    over_z(0, hops + 1, way, c).start()
                if c < X_COUNT[hops - 1]:
                    over_x(hops, way, c).start()
        if hops > 1:
            for c in range(X_COUNT[hops - 1], X_COUNT[hops - 2]):
                for way in (0, 1):
                    landed_x(hops - 1, way, c)
                    over_z(1, hops, way, c).start()
        following = X_COUNT[hops] if hops < far - 1 else 2
        for c in (3, 2):
            for way in (0, 1):
                if c >= X_COUNT[hops - 1]:
                    landed_z(1, hops, way, c)
                    if c >= following:
                        over_z(1, hops + 1, way, c).start()
        if hops == 1:
            for copy in adj_copies:
                copy.wait()
        if hops == 3:
            pl.semaphore_wait(ready.at[0], 3)
            for device in near:
                pl.semaphore_signal(ready.at[1], inc=1, device_id=device, device_id_type=MESH)
        if hops == 5:
            w_send.wait_recv()
            w_copy.wait()
            w_high, w_low = halves(w_full[...])
            w_three[...] = jnp.concatenate([w_high, w_low, w_high], axis=0)
        upto = steps * hops // (far - 1)
        split(done, upto - done)
        done = upto
    for c in (1, 2):
        own_over_x(c, partner).wait_recv()
    for hops in range(1, far):
        for c in range(X_COUNT[hops - 1]):
            for way in (0, 1):
                if hops == far - 1 or c < X_COUNT[hops]:
                    landed_x(hops, way, c)
    for copy in own_copies:
        copy.wait()
    pl.semaphore_wait(ready.at[1], 3)
    for c in (2, 3):
        for way in (0, 1):
            landed_z(0, far, way, c)
    for c in (3, 2):
        for way in (0, 1):
            landed_z(1, far, way, c)

    count = counts[0, 0]
    order = ((0, 1 - rep), (1, rep))

    def placed(side, n):
        scales = {
            k: [
                jnp.where((t < count) & (rows_at[0, 0, t] == ((y + k) % NY) * 2 + side), F32(1.0), F32(0.0))
                for t in range(4)
            ]
            for k in FAR_FIRST
        }
        for low in (0, width // 2):
            rows = pl.ds(low, width // 2)
            values = [prod[n, t, rows, :] for t in range(4)]
            for k in FAR_FIRST:
                terms = [value * scale for value, scale in zip(values, scales[k])]
                yield k, rows, low > 0, (terms[0] + terms[1]) + (terms[2] + terms[3])

    core_copies = {}
    for n, h in order:
        for t in range(4):
            nodes = pl.ds(pl.multiple_of(h * half_b, half_b), half_b)
            dims = (((1,), (1,)), ((), ()))
            if n == 0:
                high, low = halves(gath[jnp.clip(cols[0, 0, t], 0, 2 * nz - 1)])
                x_both[t] = jnp.concatenate([high, low], axis=0)
            both = lax.dot_general(x_both[t], adj_hi[t, nodes, :], dims, preferred_element_type=F32)
            rest = lax.dot_general(x_both[t, 0:width], adj_lo[t, nodes, :], dims, preferred_element_type=F32)
            prod[n, t] = both[:width] + both[width:] + rest
        for k, rows, whole, total in placed(1 - core, n):
            m_out[n, k, rows, :] = total
            if whole:
                copy = remote(m_out.at[n, k], c1_in.at[n, k], csem.at[0, n, k], csem.at[1, n, k], core_dev)
                copy.start()
                core_copies[n, k] = copy
        for k, rows, _, total in placed(core, n):
            s_buf[n, k, rows, :] = total

    y_copies = {}
    for n, k in SENDING:
        core_copies[n, k].wait_recv()
        s_buf[n, k] += c1_in[n, k]
        if (n, k) != (1, 0):
            device = {"col": ((y + k) % NY) * 2 + core, "rep": order[n][1]}
            copy = remote(s_buf.at[n, k], y_in.at[n, k], ysem.at[0, n, k], ysem.at[1, n, k], device)
            copy.start()
            y_copies[n, k] = copy
    for n, k in SENDING:
        if (n, k) in y_copies:
            y_copies[n, k].wait_recv()
    mt[pl.ds(pl.multiple_of(rep * width, width), width), :] = s_buf[1, 0] + y_in[1, 1] + y_in[1, 2] + y_in[1, 3]
    mt[pl.ds(pl.multiple_of((1 - rep) * width, width), width), :] = y_in[0, 0] + y_in[0, 1] + y_in[0, 2] + y_in[0, 3]
    mixed = mt[...]
    high, low = halves(mixed.T)
    preact = jnp.dot(jnp.concatenate([high, high, low], axis=1), w_three[...], preferred_element_type=F32) + bias[...]
    squash = 1.0 / (1.0 + jnp.exp(-preact))
    out_v[...] = preact * squash
    out_copy = pltpu.make_async_copy(out_v, out_ref, lsem.at[3])
    out_copy.start()
    slope = cot[...] * squash * (1.0 + preact * (1.0 - squash))
    high, low = halves(mixed)
    s_high, s_low = halves(slope)
    grad = jnp.dot(
        jnp.concatenate([high, high, low], axis=1),
        jnp.concatenate([s_high, s_low, s_high], axis=0),
        preferred_element_type=F32,
    )
    bias_row = jnp.sum(slope, axis=0, keepdims=True)
    for k in range(PIECES):
        g_buf[k, 0:4] = grad[4 * k : 4 * k + 4]
        g_buf[k, 4:5] = bias_row

    for i in (2, 1, 3, 0):
        for j in (4, 3, 5, 2, 6, 1, 7, 0):
            if i + j > 0:
                piece, slot_at = planes[i][0] + cols_of[j], i * 8 + j - 1
                device = {"row": planes[i][1], "rep": planes[i][2], "col": cols_of[j]}
                remote(g_buf.at[piece], f1_in.at[slot_at], fsem.at[0], fsem.at[1], device).start()
    own_piece = g_buf[planes[0][0] + col]
    remote(f1_in, f1_in, fsem.at[0], fsem.at[1], rep_dev).wait_recv()
    mine = jnp.sum(f1_in[...], axis=0) + own_piece
    p2[...] = mine
    f2_in[z] = mine
    for device in z_devs:
        remote(p2, f2_in.at[z], fsem.at[2], fsem.at[3], device).start()
    others = f2_in.at[pl.ds(0, nz - 1)]
    remote(others, others, fsem.at[2], fsem.at[3], rep_dev).wait_recv()
    mine = jnp.sum(f2_in[...], axis=0)
    p3[...] = mine[0:4]
    here = x_lo * 8 + col
    own_out = pltpu.make_async_copy(p3, gw_ref.at[here], lsem.at[8])
    for i in (1, 0):
        for j in (4, 3, 5, 2, 6, 1, 7, 0):
            if i + j > 0:
                device = {"row": (x_lo + i - 2 * i * x_lo) * nz + z, "col": cols_of[j]}
                remote(p3, gw_ref.at[here], fsem.at[4], fsem.at[5], device).start()
    own_out.start()
    bias_v[...] = mine[4:5]
    bias_out = pltpu.make_async_copy(bias_v, gb_ref, lsem.at[9])
    bias_out.start()
    f3_others = gw_ref.at[pl.ds(0, 15)]
    remote(f3_others, f3_others, fsem.at[4], fsem.at[5], rep_dev).wait()

    for copy in (out_copy, own_out, bias_out):
        copy.wait()
    part = gath.at[pl.ds(0, nz - 1)]
    remote(part, part, zs.at[0], xo.at[0], rep_dev).wait_send()
    part = gath.at[pl.ds(0, sum(4 - c for c in X_COUNT) + 2), pl.ds(0, 2 * CHUNK)]
    remote(part, part, zs.at[1], xo.at[0], rep_dev).wait_send()
    part = gath.at[pl.ds(0, sum(X_COUNT) + 2), pl.ds(0, 2 * CHUNK)]
    remote(part, part, xs.at[0], xo.at[0], rep_dev).wait_send()
    w_send.wait_send()
    for copy in (*core_copies.values(), *y_copies.values()):
        copy.wait_send()
    remote(f1_in, f1_in, fsem.at[0], fsem.at[1], rep_dev).wait_send()
    remote(others, others, fsem.at[2], fsem.at[3], rep_dev).wait_send()


def hand_over(output, grad_weight, grad_bias, out_ref, gw_ref, gb_ref):
    out_ref[...] = output[...]
    for k in range(16):
        gw_ref[4 * k : 4 * k + 4, :] = grad_weight[k]
    gb_ref[...] = grad_bias[...]


def solution(mesh):
    nz = mesh.shape["row"] // 2

    def local(adj_tiles, tile_rows, tile_cols, tile_counts, features_t, weight, bias_vec, cotangent):
        width, block = features_t.shape
        half_b = block // 2
        out_w = weight.shape[1]
        nodes = cotangent.shape[0]
        vmem = pl.BlockSpec(memory_space=pltpu.VMEM)
        hbm = pl.BlockSpec(memory_space=pltpu.HBM)
        dma = pltpu.SemaphoreType.DMA
        output, grad_weight, grad_bias = pl.pallas_call(
            functools.partial(kernel, nz),
            out_shape=(
                jax.ShapeDtypeStruct((nodes, out_w), F32),
                jax.ShapeDtypeStruct((16, width // 16, out_w), F32),
                jax.ShapeDtypeStruct((1, out_w), F32),
            ),
            in_specs=[hbm] * 8,
            out_specs=(hbm,) * 3,
            scratch_shapes=[
                pltpu.SMEM(tile_rows.shape, jnp.int32),
                pltpu.SMEM(tile_cols.shape, jnp.int32),
                pltpu.SMEM(tile_counts.shape, jnp.int32),
                pltpu.VMEM((1, out_w), F32),
                pltpu.VMEM((2 * nz, width, block), F32),
                pltpu.VMEM((4, block, block), F32),
                pltpu.VMEM((4, block, block), BF16),
                pltpu.VMEM((4, block, block), BF16),
                pltpu.VMEM((2, 4, width, half_b), F32),
                pltpu.VMEM((2, 4, width, half_b), F32),
                pltpu.VMEM((2, 4, width, half_b), F32),
                pltpu.VMEM((2, 4, width, half_b), F32),
                pltpu.VMEM((2, 4, width, half_b), F32),
                pltpu.VMEM((2 * width, half_b), F32),
                pltpu.VMEM((2 * width, out_w), F32),
                pltpu.VMEM((6 * width, out_w), BF16),
                pltpu.VMEM((4, 2 * width, block), BF16),
                pltpu.VMEM((nodes, out_w), F32),
                pltpu.VMEM((nodes, out_w), F32),
                pltpu.VMEM((PIECES, 5, out_w), F32),
                pltpu.VMEM((PIECES - 1, 5, out_w), F32),
                pltpu.VMEM((nz, 5, out_w), F32),
                pltpu.VMEM((5, out_w), F32),
                pltpu.VMEM((4, out_w), F32),
                pltpu.VMEM((1, out_w), F32),
                dma((2, nz // 2, 6)),
                dma((2, nz // 2 - 1, 3)),
                dma((4,)),
                dma((2,)),
                dma((1,)),
                dma((10,)),
                dma((4,)),
                dma((2,)),
                dma((2, 2, 4)),
                dma((2, 2, 4)),
                dma((6,)),
                pltpu.SemaphoreType.REGULAR((2,)),
            ],
            compiler_params=pltpu.CompilerParams(
                collective_id=0, has_side_effects=True, vmem_limit_bytes=67043328
            ),
        )(tile_rows, tile_cols, tile_counts, adj_tiles, features_t, weight, bias_vec.reshape(1, out_w), cotangent)
        output, grad_weight, grad_bias = pl.pallas_call(
            hand_over,
            out_shape=tuple(
                jax.ShapeDtypeStruct(shape, F32) for shape in (output.shape, (width, out_w), grad_bias.shape)
            ),
            in_specs=[vmem] * 3,
            out_specs=(vmem,) * 3,
        )(output, grad_weight, grad_bias)
        return output, grad_weight, grad_bias.reshape(out_w)

    return jax.shard_map(
        local,
        mesh=mesh,
        in_specs=(
            P("row", "col", None, None, None),
            P("row", "col", None),
            P("row", "col", None),
            P("row", "col"),
            P("rep", ("row", "col")),
            P("rep", None),
            P(),
            P(("row", "col", "rep"), None),
        ),
        out_specs=(P(("row", "col", "rep"), None), P("rep", None), P()),
        check_vma=False,
    )
```
